128 devices in a mesh: view: 2 (over y_hi), block: 64 (over y_lo, x, z, core).
Axes of the slice: x: 4, y: 4 (y_hi: 2, y_lo: 2; y = y_hi * 2 + y_lo), z: 4, core: 2. Of those that a mesh axis runs over, the one named last changes fastest.
Arguments:
- estimate: float32 [2048, 128, 128], P('block'), may hold values from 0.5 to 2
- view_tiles: bfloat16 [2, 1536, 4, 128, 128], P('view', 'block'), may hold values from 0.25 to 4
- tile_dest: int32 [2, 1536, 3], P('view', 'block'), may hold values from 0 to 63, as said below
- psf_taps: float32 [6, 3, 31], P('view'), may hold values from 0.05 to 1
Outputs:
- deblurred: float32 [2048, 128, 128], P('block')
The draws below stay inside these ranges and needn't reach their ends.
Inputs may be any that keep to these rules, and one draw needn't show every extreme that they name: `tile_dest`: for each index of view, every triple of owner block, view within the index and tile position appears in exactly one row. The rows of block device s send exactly 2 tiles to each owner (s + d) mod 64 for d from -(6) to 5, and none elsewhere, in any order.
All inputs are finite; a program needn't handle non-finite values.
Results may differ from the reference program's by a relative error of at most 0.0003.
Values may be sent and summed in bfloat16 or wider, within the bound.
No kernel may reach another device: no remote copies, remote signals or barrier semaphores. Data moves between devices by JAX's collectives and lax.ppermute only.
A program may use at most 192 MiB of HBM per device.

```python
import math
import jax
import jax.numpy as jnp
from jax import lax

TAPS = 31
BX = 32
Y = 128
Z = 128
VIEWS_DEV = 3
ITERS = 2
CAP = 2
SPAN = 12
TP = 4
SLOTS = 24
VIEWS = 6
X = 2048
TILES = 1536
N_VIEW = 2
N_BLOCK = 64


def draw_tile_dest(key, part):
    per_block = BX // TP

    def one_view(view_key):
        first_key, second_key = jax.random.split(view_key)
        offsets = jnp.arange(SPAN, dtype=jnp.int32) - SPAN // 2
        source = jnp.arange(N_BLOCK, dtype=jnp.int32)[:, None, None]
        owner_ids = (source + offsets[None, :, None]) % N_BLOCK
        owner_ids = jnp.broadcast_to(owner_ids, (N_BLOCK, SPAN, CAP))
        slot_ids = jnp.arange(SPAN, dtype=jnp.int32)[:, None] * CAP + jnp.arange(CAP, dtype=jnp.int32)[None, :]
        slot_ids = jnp.broadcast_to(slot_ids[None, :, :], owner_ids.shape)
        item_perm = jax.vmap(lambda sub_key: jax.random.permutation(sub_key, SLOTS))(jax.random.split(first_key, N_BLOCK))
        items = item_perm[owner_ids, slot_ids]
        stacked = jnp.stack([owner_ids, items // per_block, items % per_block], axis=-1).reshape(N_BLOCK, SLOTS, 3)
        row_perm = jax.vmap(lambda sub_key: jax.random.permutation(sub_key, SLOTS))(jax.random.split(second_key, N_BLOCK))
        stacked = jnp.take_along_axis(stacked, row_perm[:, :, None].astype(jnp.int32), axis=1)
        return stacked.reshape(N_BLOCK * SLOTS, 3).astype(jnp.int32)
    view_keys = jax.random.split(jax.random.fold_in(key, 11), N_VIEW)
    return jax.vmap(one_view)(view_keys)


def level_of(stream_key, extent, cuts, least, largest):
    loudness, own = 1.0, jax.random.fold_in(stream_key, 6)
    for position, blocks in cuts:
        steps = jnp.exp(jax.random.uniform(jax.random.fold_in(own, position), (blocks,), jnp.float32, least / len(cuts), largest / len(cuts)))
        loudness = loudness * jnp.repeat(steps, extent[position] // blocks).reshape([-1 if axis == position else 1 for axis in range(len(extent))])
    return loudness


def setup_inputs(seed: int = 0) -> dict:
    keys = jax.random.split(jax.random.key(seed), 5)
    return {
        "estimate": jnp.clip(jnp.exp(math.log(2.0) - 1.3862944 * jax.random.uniform(keys[0], (X, Y, Z), jnp.float32) ** level_of(keys[0], (X, Y, Z), ((0, 64),), -0.2, 0.2)), 0.5, 2.0),
        "view_tiles": jnp.clip(jnp.exp(math.log(4.0) - 2.7725887 * jax.random.uniform(keys[1], (N_VIEW, TILES, TP, Y, Z), jnp.float32) ** level_of(keys[1], (N_VIEW, TILES, TP, Y, Z), ((0, 2), (1, 64)), -0.2, 0.2)), 0.25, 4.0).astype(jnp.bfloat16),
        "tile_dest": draw_tile_dest(jax.random.fold_in(keys[4], 71), 0),
        "psf_taps": jnp.clip(jnp.exp(math.log(1.0) - 2.9957323 * jax.random.uniform(keys[3], (VIEWS, 3, TAPS), jnp.float32) ** level_of(keys[3], (VIEWS, 3, TAPS), ((0, 2),), -0.2, 0.2)), 0.05, 1.0),
    }


def banded(kernel, rows, cols, sign, offset):
    row_idx = jnp.arange(rows)[:, None]
    col_idx = jnp.arange(cols)[None, :]
    lag = sign * (col_idx - row_idx) + offset
    hits = (lag[:, :, None] == jnp.arange(kernel.shape[-1])[None, None, :]).astype(jnp.float32)
    return jnp.einsum('t,ijt->ij', kernel, hits, precision=lax.Precision.HIGHEST)


def blur_view(volume, kernel, forward):
    half_width = TAPS // 2
    count = volume.shape[0]
    padded = jnp.pad(volume, ((half_width, half_width), (0, 0), (0, 0)))
    total = jnp.zeros_like(volume)
    for tap in range(TAPS):
        if forward:
            total = total + kernel[0, tap] * padded[tap:tap + count]
        else:
            begin = 2 * half_width - tap
            total = total + kernel[0, tap] * padded[begin:begin + count]
    sign = 1 if forward else -1
    along_y = banded(kernel[1], Y, Y, sign, half_width)
    along_z = banded(kernel[2], Z, Z, sign, half_width)
    total = jnp.einsum('ij,xjz->xiz', along_y, total, precision=lax.Precision.HIGHEST)
    total = jnp.einsum('xyj,ij->xyi', total, along_z, precision=lax.Precision.HIGHEST)
    return total


def reference(estimate, view_tiles, tile_dest, psf_taps):
    kernels = psf_taps / jnp.sum(psf_taps, axis=-1, keepdims=True)
    view_dev = jnp.broadcast_to(jnp.arange(N_VIEW, dtype=jnp.int32)[:, None], tile_dest.shape[:2])
    view_ids = (view_dev * VIEWS_DEV + tile_dest[:, :, 1]).astype(jnp.int32).reshape(-1)
    plane_ids = (tile_dest[:, :, 0] * (BX // TP) + tile_dest[:, :, 2]).astype(jnp.int32).reshape(-1)
    measured = jnp.zeros((VIEWS, X // TP, TP, Y, Z), jnp.bfloat16)
    measured = measured.at[view_ids, plane_ids].set(view_tiles.reshape(-1, TP, Y, Z))
    measured = measured.reshape(VIEWS, X, Y, Z)
    deblurred = estimate
    for sweep in range(ITERS):
        total = jnp.zeros_like(estimate)
        for view in range(VIEWS):
            blurred = blur_view(deblurred, kernels[view], True)
            ratios = measured[view].astype(jnp.float32) / blurred
            total = total + blur_view(ratios, kernels[view], False)
        deblurred = deblurred * total / VIEWS
    return deblurred
```

```python
import functools

import jax
import jax.numpy as jnp
from jax import lax
from jax.experimental import pallas as pl
from jax.experimental.pallas import tpu as pltpu
from jax.sharding import PartitionSpec as P

TAPS = 31
HALF = TAPS // 2
BX = 32
HX = 16
EX = BX + 2 * HX
Y = 128
Z = 128
VIEWS_DEV = 3
ITERS = 2
CAP = 2
SPAN = 12
TP = 4
SLOTS = SPAN * CAP
TROWS = TP * Y
PROWS = CAP * TROWS + 16
SUB = 16
F32 = jnp.float32
BF16 = jnp.bfloat16
VMEM_LIMIT = 56 << 20


def banded(kernel, rows, cols, sign, offset):
    row_idx = jnp.arange(rows)[:, None]
    col_idx = jnp.arange(cols)[None, :]
    lag = sign * (col_idx - row_idx) + offset
    hits = (lag[:, :, None] == jnp.arange(kernel.shape[-1])[None, None, :]).astype(F32)
    return jnp.einsum("vt,ijt->vij", kernel, hits, precision=lax.Precision.HIGHEST)


def rounded(value):
    return lax.reduce_precision(value, 8, 7)


def two_terms(matrix, axis):
    high = rounded(matrix)
    return jnp.concatenate([high, matrix - high], axis=axis).astype(BF16)


def blur_matrices(kernels):
    taps_x = rounded(kernels[:, 0])
    taps_y = kernels[:, 1] * (jnp.sum(kernels[:, 0], -1) / jnp.sum(taps_x, -1))[:, None]
    taps_z = kernels[:, 2]
    small = banded(taps_x, BX, EX, 1, -1)
    eye = jnp.eye(SUB, dtype=F32)
    fwd_x = (small[:, :, None, :, None] * eye[None, None, :, None, :]).reshape(
        VIEWS_DEV * BX * SUB, EX * SUB
    )
    flipped = jnp.transpose(small, (2, 0, 1))
    back_x = (flipped[:, None, :, :, None] * eye[None, :, None, None, :]).reshape(
        EX * SUB, VIEWS_DEV * BX * SUB
    )
    y_fwd = banded(taps_y, Y, Y, 1, HALF)
    y_back = banded(taps_y, Y, Y, -1, HALF)
    z_fwd = banded(taps_z, Z, Z, -1, HALF)
    z_back = banded(taps_z, Z, Z, 1, HALF)
    return (
        (fwd_x.astype(BF16), two_terms(y_fwd, 2), two_terms(z_fwd, 1)),
        (back_x.astype(BF16), two_terms(y_back, 2), two_terms(z_back, 1)),
    )


def pack_kernel(me_ref, dest_ref, tiles_ref, *refs):
    outs, (order_ref, count_ref) = refs[:SPAN], refs[SPAN:]
    me = me_ref[0]
    for k in range(SPAN):
        count_ref[k] = 0
    for n in range(SLOTS):
        step = lax.rem(dest_ref[n, 0] - me + SPAN // 2 + 64, 64)
        rank = count_ref[step]
        count_ref[step] = rank + 1
        order_ref[step * CAP + rank] = n
    for k in range(SPAN):
        codes = []
        for c in range(CAP):
            n = order_ref[k * CAP + c]
            outs[k][c * TROWS : (c + 1) * TROWS, :] = tiles_ref[n]
            code = dest_ref[n, 1] * (BX // TP) + dest_ref[n, 2]
            codes.append(jnp.full((8, Z), code, jnp.int32).astype(F32))
        outs[k][CAP * TROWS :, :] = jnp.concatenate(codes, axis=0).astype(BF16)


def pack_tiles(view_tiles, tile_dest):
    me = lax.axis_index("block").astype(jnp.int32).reshape(1)
    return pl.pallas_call(
        pack_kernel,
        out_shape=[jax.ShapeDtypeStruct((PROWS, Z), BF16)] * SPAN,
        in_specs=[
            pl.BlockSpec(memory_space=pltpu.SMEM),
            pl.BlockSpec(memory_space=pltpu.SMEM),
            pl.BlockSpec(memory_space=pltpu.VMEM),
        ],
        out_specs=[pl.BlockSpec(memory_space=pltpu.VMEM)] * SPAN,
        scratch_shapes=[pltpu.SMEM((SLOTS,), jnp.int32), pltpu.SMEM((SPAN,), jnp.int32)],
        compiler_params=pltpu.CompilerParams(vmem_limit_bytes=VMEM_LIMIT),
        cost_estimate=pl.CostEstimate(flops=0, bytes_accessed=2 * SLOTS * TROWS * Z * 2, transcendentals=0),
        name="pack_tiles",
    )(me, tile_dest[0], view_tiles.reshape(SLOTS, TROWS, Z))


def side_by_side(ref, y0):
    planes = ref.shape[0]
    return jnp.concatenate(
        [ref[:, pl.ds(y0 + h * SUB, SUB), :].reshape(planes * SUB, Z) for h in range(2)], axis=1
    )


def blur_into(kx_ref, ky_ref, kz_ref, parts, half_ref, out_ref):
    def along_x(t, carry):
        y0 = pl.multiple_of(t * 2 * SUB, 2 * SUB)
        data = jnp.concatenate([side_by_side(ref, y0) for ref in parts], axis=0)
        for v in range(VIEWS_DEV):
            rows = slice(v * BX * SUB, (v + 1) * BX * SUB)
            got = jnp.dot(kx_ref[rows, :], data, preferred_element_type=F32).astype(BF16)
            for h in range(2):
                half_ref[v * BX : (v + 1) * BX, pl.ds(y0 + h * SUB, SUB), :] = got[
                    :, h * Z : (h + 1) * Z
                ].reshape(BX, SUB, Z)
        return carry

    lax.fori_loop(0, Y // (2 * SUB), along_x, 0)

    def along_yz(q, carry):
        v = q // (BX // TP)
        planes = [half_ref[q * TP + i] for i in range(TP)]
        outs = []
        for i in range(0, TP, 2):
            pair = jnp.concatenate(planes[i : i + 2], axis=1)
            got = jnp.dot(
                ky_ref[v], jnp.concatenate([pair, pair], axis=0), preferred_element_type=F32
            ).astype(BF16)
            outs += [got[:, :Z], got[:, Z:]]
        rows = jnp.concatenate(outs, axis=0)
        out_ref[q] = jnp.dot(
            jnp.concatenate([rows, rows], axis=1), kz_ref[v], preferred_element_type=F32
        )
        return carry

    lax.fori_loop(0, VIEWS_DEV * BX // TP, along_yz, 0)


def back_from(kx_ref, ky_ref, kz_ref, measured_ref, blurred_ref, half_ref, outs):
    def along_zy(q, carry):
        v = q // (BX // TP)
        ratio = (measured_ref[q].astype(F32) / blurred_ref[q]).astype(BF16)
        rows = jnp.dot(
            jnp.concatenate([ratio, ratio], axis=1), kz_ref[v], preferred_element_type=F32
        ).astype(BF16)
        for i in range(0, TP, 2):
            pair = jnp.concatenate([rows[(i + j) * Y : (i + j + 1) * Y] for j in range(2)], axis=1)
            got = jnp.dot(
                ky_ref[v], jnp.concatenate([pair, pair], axis=0), preferred_element_type=F32
            )
            high = got.astype(BF16)
            low = (got - high.astype(F32)).astype(BF16)
            for j in range(2):
                half_ref[0, q * TP + i + j] = high[:, j * Z : (j + 1) * Z]
                half_ref[1, q * TP + i + j] = low[:, j * Z : (j + 1) * Z]
        return carry

    lax.fori_loop(0, VIEWS_DEV * BX // TP, along_zy, 0)

    def along_x(t, carry):
        y0 = pl.multiple_of(t * 2 * SUB, 2 * SUB)
        high = side_by_side(half_ref.at[0], y0)
        low = side_by_side(half_ref.at[1], y0)
        first = 0
        for ref in outs:
            count = ref.shape[0]
            taps = kx_ref[first * SUB : (first + count) * SUB, :]
            got = jnp.dot(taps, high, preferred_element_type=F32)
            got += jnp.dot(taps, low, preferred_element_type=F32)
            for h in range(2):
                ref[:, pl.ds(y0 + h * SUB, SUB), :] = got[:, h * Z : (h + 1) * Z].reshape(
                    count, SUB, Z
                )
            first += count
        return carry

    lax.fori_loop(0, Y // (2 * SUB), along_x, 0)


def first_blur_kernel(kx_ref, ky_ref, kz_ref, left_ref, mid_ref, right_ref, out_ref, half_ref):
    blur_into(kx_ref, ky_ref, kz_ref, (left_ref, mid_ref, right_ref), half_ref, out_ref)


def first_back_kernel(kx_ref, ky_ref, kz_ref, blurred_ref, *refs):
    tiles = refs[:SPAN]
    left_ref, mid_ref, right_ref, measured_ref, half_ref = refs[SPAN:]
    for k in range(SPAN):
        for c in range(CAP):
            code = tiles[k][CAP * TROWS :, :].astype(F32)[8 * c, 0].astype(jnp.int32)
            measured_ref[code] = tiles[k][c * TROWS : (c + 1) * TROWS, :]
    back_from(
        kx_ref, ky_ref, kz_ref, measured_ref, blurred_ref, half_ref, (left_ref, mid_ref, right_ref)
    )


def sweep_kernel(*refs):
    fwd, back, parts = refs[0:3], refs[3:6], refs[6:9]
    measured_ref = refs[9]
    outs = refs[10:13]
    half_ref, back_half_ref, blurred_ref = refs[13:]
    blur_into(*fwd, parts, half_ref, blurred_ref)
    back_from(*back, measured_ref, blurred_ref, back_half_ref, outs)


VM = pl.BlockSpec(memory_space=pltpu.VMEM)
BLURRED = (VIEWS_DEV * BX // TP, TROWS, Z)
HALF_SHAPE = (VIEWS_DEV * BX, Y, Z)
CONTRIB = [jax.ShapeDtypeStruct((n, Y, Z), F32) for n in (HX, BX, HX)]


def call(kernel, name, operands, out_shape, scratch, flops):
    return pl.pallas_call(
        kernel,
        out_shape=out_shape,
        in_specs=[VM] * len(operands),
        out_specs=jax.tree.map(lambda _: VM, out_shape),
        scratch_shapes=scratch,
        compiler_params=pltpu.CompilerParams(vmem_limit_bytes=VMEM_LIMIT),
        cost_estimate=pl.CostEstimate(flops=flops, bytes_accessed=12 << 20, transcendentals=0),
        name=name,
    )(*operands)


def neighbours(low, high):
    size = lax.axis_size("block")
    up = [(i, i + 1) for i in range(size - 1)]
    down = [(j, i) for i, j in up]
    return lax.ppermute(high, "block", up), lax.ppermute(low, "block", down)


def with_halo(estimate):
    planes = estimate.astype(BF16)
    left, right = neighbours(planes[:HX], planes[HX:])
    return left, planes, right


def updated(estimate, contributions, view_count):
    left, mid, right = contributions
    from_left, from_right = neighbours(left, right)
    partial = mid + jnp.concatenate([from_left, from_right], axis=0)
    other = lax.ppermute(partial, "view", [(0, 1), (1, 0)])
    return estimate * (partial + other) / view_count


def shards(estimate, view_tiles, tile_dest, psf_taps):
    kernels = psf_taps / jnp.sum(psf_taps, axis=-1, keepdims=True)
    view_count = kernels.shape[0] * lax.axis_size("view")
    blocks = lax.axis_size("block")
    packed = pack_tiles(view_tiles, tile_dest)
    arrived = []
    for k in range(SPAN):
        by = k - SPAN // 2
        perm = [(i, (i + by) % blocks) for i in range(blocks)]
        arrived.append(lax.ppermute(packed[k], "block", perm) if by else packed[k])
    fwd, back = blur_matrices(kernels)
    blurred = call(
        first_blur_kernel,
        "first_blur",
        (*fwd, *with_halo(estimate)),
        jax.ShapeDtypeStruct(BLURRED, F32),
        [pltpu.VMEM(HALF_SHAPE, BF16)],
        6 << 30,
    )
    *contributions, measured = call(
        first_back_kernel,
        "first_back",
        (*back, blurred, *arrived),
        [*CONTRIB, jax.ShapeDtypeStruct((VIEWS_DEV * BX // TP, TROWS, Z), BF16)],
        [pltpu.VMEM((2, *HALF_SHAPE), BF16)],
        8 << 30,
    )
    estimate = updated(estimate, contributions, view_count)
    contributions = call(
        sweep_kernel,
        "sweep",
        (*fwd, *back, *with_halo(estimate), measured),
        CONTRIB,
        [
            pltpu.VMEM(HALF_SHAPE, BF16),
            pltpu.VMEM((2, *HALF_SHAPE), BF16),
            pltpu.VMEM(BLURRED, F32),
        ],
        14 << 30,
    )
    return updated(estimate, contributions, view_count)


def solution(mesh):
    return jax.shard_map(
        shards,
        mesh=mesh,
        in_specs=(
            P("block", None, None),
            P("view", "block", None, None, None),
            P("view", "block", None),
            P("view", None, None),
        ),
        out_specs=P("block", None, None),
        check_vma=False,
    )
```

```python
import functools

import jax
import jax.numpy as jnp
from jax import lax
from jax.experimental import pallas as pl
from jax.experimental.pallas import tpu as pltpu
from jax.sharding import PartitionSpec as P

TAPS = 31
HALF = TAPS // 2
BX = 32
HX = 16
EX = BX + 2 * HX
Y = 128
Z = 128
VIEWS_DEV = 3
ITERS = 2
CAP = 2
SPAN = 12
TP = 4
SLOTS = SPAN * CAP
TROWS = TP * Y
PROWS = CAP * TROWS + 16
SUB = 16
F32 = jnp.float32
BF16 = jnp.bfloat16
VMEM_LIMIT = 56 << 20
UNROLL = 2


def banded(kernel, rows, cols, sign, offset):
    row_idx = jnp.arange(rows)[:, None]
    col_idx = jnp.arange(cols)[None, :]
    lag = sign * (col_idx - row_idx) + offset
    hits = (lag[:, :, None] == jnp.arange(kernel.shape[-1])[None, None, :]).astype(F32)
    return jnp.einsum("vt,ijt->vij", kernel, hits, precision=lax.Precision.HIGHEST)


def rounded(value):
    return lax.reduce_precision(value, 8, 7)


def two_terms(matrix, axis):
    high = rounded(matrix)
    return jnp.concatenate([high, matrix - high], axis=axis).astype(BF16)


def blur_matrices(kernels):
    taps_x, taps_y, taps_z = kernels[:, 0], kernels[:, 1], kernels[:, 2]
    near_x = rounded(taps_x)
    back_y = taps_y * (jnp.sum(taps_x, -1) / jnp.sum(near_x, -1))[:, None]
    fwd_x = banded(taps_x, BX, EX, 1, -1).reshape(VIEWS_DEV * BX, EX)
    back_x = jnp.transpose(banded(near_x, BX, EX, 1, -1).reshape(VIEWS_DEV * BX, EX))
    back_x = jnp.concatenate([back_x, back_x], axis=1).astype(BF16)
    y_fwd = banded(taps_y, Y, Y, 1, HALF)
    y_back = banded(back_y, Y, Y, -1, HALF)
    z_fwd = banded(taps_z, Z, Z, -1, HALF)
    z_back = banded(taps_z, Z, Z, 1, HALF)
    return (
        (two_terms(fwd_x, 1), two_terms(y_fwd, 2), two_terms(z_fwd, 1)),
        (back_x, two_terms(y_back, 2), two_terms(z_back, 1)),
    )


def pack_kernel(me_ref, dest_ref, tiles_ref, *refs):
    outs, (order_ref, count_ref) = refs[:SPAN], refs[SPAN:]
    me = me_ref[0]
    for k in range(SPAN):
        count_ref[k] = 0
    for n in range(SLOTS):
        step = lax.rem(dest_ref[n, 0] - me + SPAN // 2 + 64, 64)
        rank = count_ref[step]
        count_ref[step] = rank + 1
        order_ref[step * CAP + rank] = n
    for k in range(SPAN):
        codes = []
        for c in range(CAP):
            n = order_ref[k * CAP + c]
            outs[k][c * TROWS : (c + 1) * TROWS, :] = tiles_ref[n]
            code = dest_ref[n, 1] * (BX // TP) + dest_ref[n, 2]
            codes.append(jnp.full((8, Z), code, jnp.int32).astype(F32))
        outs[k][CAP * TROWS :, :] = jnp.concatenate(codes, axis=0).astype(BF16)


def pack_tiles(view_tiles, tile_dest):
    me = lax.axis_index("block").astype(jnp.int32).reshape(1)
    return pl.pallas_call(
        pack_kernel,
        out_shape=[jax.ShapeDtypeStruct((PROWS, Z), BF16)] * SPAN,
        in_specs=[
            pl.BlockSpec(memory_space=pltpu.SMEM),
            pl.BlockSpec(memory_space=pltpu.SMEM),
            pl.BlockSpec(memory_space=pltpu.VMEM),
        ],
        out_specs=[pl.BlockSpec(memory_space=pltpu.VMEM)] * SPAN,
        scratch_shapes=[pltpu.SMEM((SLOTS,), jnp.int32), pltpu.SMEM((SPAN,), jnp.int32)],
        compiler_params=pltpu.CompilerParams(vmem_limit_bytes=VMEM_LIMIT),
        cost_estimate=pl.CostEstimate(flops=0, bytes_accessed=2 * SLOTS * TROWS * Z * 2, transcendentals=0),
        name="pack_tiles",
    )(me, tile_dest[0], view_tiles.reshape(SLOTS, TROWS, Z))


def swapped(block):
    return jnp.transpose(block, (1, 0, 2))


def blur_into(kx_ref, ky_ref, kz_ref, parts, half_ref, out_ref):
    def along_x(t, carry):
        y0 = pl.multiple_of(t * SUB, SUB)
        data = jnp.concatenate([ref[:, pl.ds(y0, SUB), :] for ref in parts], axis=0).astype(F32)
        for h in range(0, SUB, 8):
            rows = swapped(data[:, h : h + 8]).astype(BF16)
            outs = []
            for j in range(0, 8, 2):
                pair = jnp.concatenate([rows[j], rows[j + 1]], axis=1)
                got = jnp.dot(
                    kx_ref[...], jnp.concatenate([pair, pair], axis=0), preferred_element_type=F32
                )
                outs += [got[:, :Z], got[:, Z:]]
            half_ref[:, pl.ds(y0 + h, 8), :] = swapped(jnp.stack(outs, axis=0))
        return carry

    lax.fori_loop(0, Y // SUB, along_x, 0)

    def along_yz(q, carry):
        v = q // (BX // TP)
        outs = []
        for i in range(0, TP, 2):
            pair = jnp.concatenate(
                [half_ref[q * TP + i + j].astype(BF16) for j in range(2)], axis=1
            )
            got = jnp.dot(
                ky_ref[v], jnp.concatenate([pair, pair], axis=0), preferred_element_type=F32
            ).astype(BF16)
            outs += [got[:, :Z], got[:, Z:]]
        rows = jnp.concatenate(outs, axis=0)
        out_ref[q] = jnp.dot(
            jnp.concatenate([rows, rows], axis=1), kz_ref[v], preferred_element_type=F32
        )
        return carry

    lax.fori_loop(0, VIEWS_DEV * BX // TP, along_yz, 0, unroll=UNROLL)


def back_from(kx_ref, ky_ref, kz_ref, measured_ref, blurred_ref, half_ref, outs):
    def along_zy(q, carry):
        v = q // (BX // TP)
        ratio = (measured_ref[q].astype(F32) / blurred_ref[q]).astype(BF16)
        rows = jnp.dot(
            jnp.concatenate([ratio, ratio], axis=1), kz_ref[v], preferred_element_type=F32
        ).astype(BF16)
        for i in range(0, TP, 2):
            pair = jnp.concatenate([rows[(i + j) * Y : (i + j + 1) * Y] for j in range(2)], axis=1)
            got = jnp.dot(
                ky_ref[v], jnp.concatenate([pair, pair], axis=0), preferred_element_type=F32
            )
            for j in range(2):
                half_ref[q * TP + i + j] = got[:, j * Z : (j + 1) * Z]
        return carry

    lax.fori_loop(0, VIEWS_DEV * BX // TP, along_zy, 0, unroll=UNROLL)

    def along_x(t, carry):
        y0 = pl.multiple_of(t * 8, 8)
        data = swapped(half_ref[:, pl.ds(y0, 8), :])
        high = data.astype(BF16)
        low = (data - high.astype(F32)).astype(BF16)
        got = []
        for j in range(0, 8, 2):
            pair = [jnp.concatenate([part[j], part[j + 1]], axis=1) for part in (high, low)]
            both = jnp.dot(
                kx_ref[...], jnp.concatenate(pair, axis=0), preferred_element_type=F32
            )
            got += [both[:, :Z], both[:, Z:]]
        planes = swapped(jnp.stack(got, axis=0))
        first = 0
        for ref in outs:
            count = ref.shape[0]
            ref[:, pl.ds(y0, 8), :] = planes[first : first + count]
            first += count
        return carry

    lax.fori_loop(0, Y // 8, along_x, 0, unroll=UNROLL)


def first_blur_kernel(kx_ref, ky_ref, kz_ref, left_ref, mid_ref, right_ref, out_ref, half_ref):
    blur_into(kx_ref, ky_ref, kz_ref, (left_ref, mid_ref, right_ref), half_ref, out_ref)


def first_back_kernel(kx_ref, ky_ref, kz_ref, blurred_ref, *refs):
    tiles = refs[:SPAN]
    left_ref, mid_ref, right_ref, measured_ref, half_ref = refs[SPAN:]
    for k in range(SPAN):
        for c in range(CAP):
            code = tiles[k][CAP * TROWS :, :].astype(F32)[8 * c, 0].astype(jnp.int32)
            measured_ref[code] = tiles[k][c * TROWS : (c + 1) * TROWS, :]
    back_from(
        kx_ref, ky_ref, kz_ref, measured_ref, blurred_ref, half_ref, (left_ref, mid_ref, right_ref)
    )


def sweep_kernel(*refs):
    fwd, back, parts = refs[0:3], refs[3:6], refs[6:9]
    measured_ref = refs[9]
    outs = refs[10:13]
    half_ref, back_half_ref, blurred_ref = refs[13:]
    blur_into(*fwd, parts, half_ref, blurred_ref)
    back_from(*back, measured_ref, blurred_ref, back_half_ref, outs)


VM = pl.BlockSpec(memory_space=pltpu.VMEM)
BLURRED = (VIEWS_DEV * BX // TP, TROWS, Z)
HALF_SHAPE = (VIEWS_DEV * BX, Y, Z)
CONTRIB = [jax.ShapeDtypeStruct((n, Y, Z), F32) for n in (HX, BX, HX)]


def call(kernel, name, operands, out_shape, scratch, flops):
    return pl.pallas_call(
        kernel,
        out_shape=out_shape,
        in_specs=[VM] * len(operands),
        out_specs=jax.tree.map(lambda _: VM, out_shape),
        scratch_shapes=scratch,
        compiler_params=pltpu.CompilerParams(vmem_limit_bytes=VMEM_LIMIT),
        cost_estimate=pl.CostEstimate(flops=flops, bytes_accessed=12 << 20, transcendentals=0),
        name=name,
    )(*operands)


def neighbours(low, high):
    size = lax.axis_size("block")
    up = [(i, i + 1) for i in range(size - 1)]
    down = [(j, i) for i, j in up]
    return lax.ppermute(high, "block", up), lax.ppermute(low, "block", down)


def with_halo(estimate):
    planes = estimate.astype(BF16)
    left, right = neighbours(planes[:HX], planes[HX:])
    return left, planes, right


def updated(estimate, contributions, view_count):
    left, mid, right = contributions
    from_left, from_right = neighbours(left, right)
    partial = mid + jnp.concatenate([from_left, from_right], axis=0)
    other = lax.ppermute(partial, "view", [(0, 1), (1, 0)])
    return estimate * (partial + other) / view_count


def shards(estimate, view_tiles, tile_dest, psf_taps):
    kernels = psf_taps / jnp.sum(psf_taps, axis=-1, keepdims=True)
    view_count = kernels.shape[0] * lax.axis_size("view")
    blocks = lax.axis_size("block")
    packed = pack_tiles(view_tiles, tile_dest)
    arrived = []
    for k in range(SPAN):
        by = k - SPAN // 2
        perm = [(i, (i + by) % blocks) for i in range(blocks)]
        arrived.append(lax.ppermute(packed[k], "block", perm) if by else packed[k])
    fwd, back = blur_matrices(kernels)
    blurred = call(
        first_blur_kernel,
        "first_blur",
        (*fwd, *with_halo(estimate)),
        jax.ShapeDtypeStruct(BLURRED, F32),
        [pltpu.VMEM(HALF_SHAPE, F32)],
        6 << 30,
    )
    *contributions, measured = call(
        first_back_kernel,
        "first_back",
        (*back, blurred, *arrived),
        [*CONTRIB, jax.ShapeDtypeStruct((VIEWS_DEV * BX // TP, TROWS, Z), BF16)],
        [pltpu.VMEM(HALF_SHAPE, F32)],
        8 << 30,
    )
    estimate = updated(estimate, contributions, view_count)
    contributions = call(
        sweep_kernel,
        "sweep",
        (*fwd, *back, *with_halo(estimate), measured),
        CONTRIB,
        [
            pltpu.VMEM(HALF_SHAPE, F32),
            pltpu.VMEM(HALF_SHAPE, F32),
            pltpu.VMEM(BLURRED, F32),
        ],
        14 << 30,
    )
    return updated(estimate, contributions, view_count)


def solution(mesh):
    return jax.shard_map(
        shards,
        mesh=mesh,
        in_specs=(
            P("block", None, None),
            P("view", "block", None, None, None),
            P("view", "block", None),
            P("view", None, None),
        ),
        out_specs=P("block", None, None),
        check_vma=False,
    )
```

```python
import functools

import jax
import jax.numpy as jnp
from jax import lax
from jax.experimental import pallas as pl
from jax.experimental.pallas import tpu as pltpu
from jax.sharding import PartitionSpec as P

TAPS = 31
HALF = TAPS // 2
BX = 32
HX = 16
EX = BX + 2 * HX
Y = 128
Z = 128
VIEWS_DEV = 3
ITERS = 2
CAP = 2
SPAN = 12
TP = 4
SLOTS = SPAN * CAP
TROWS = TP * Y
PROWS = CAP * TROWS + 16
SUB = 16
F32 = jnp.float32
BF16 = jnp.bfloat16
F16 = jnp.float16
VMEM_LIMIT = 56 << 20
UNROLL = 2
LEVELS = 7


def banded(kernel, rows, cols, sign, offset):
    row_idx = jnp.arange(rows)[:, None]
    col_idx = jnp.arange(cols)[None, :]
    lag = sign * (col_idx - row_idx) + offset
    hits = (lag[:, :, None] == jnp.arange(kernel.shape[-1])[None, None, :]).astype(F32)
    return jnp.einsum("vt,ijt->vij", kernel, hits, precision=lax.Precision.HIGHEST)


def rounded(value):
    return lax.reduce_precision(value, 8, 7)


def two_terms(matrix, axis):
    high = rounded(matrix)
    return jnp.concatenate([high, matrix - high], axis=axis).astype(BF16)


def blur_matrices(kernels):
    taps_x, taps_y, taps_z = kernels[:, 0], kernels[:, 1], kernels[:, 2]
    near_x = rounded(taps_x)
    back_y = taps_y * (jnp.sum(taps_x, -1) / jnp.sum(near_x, -1))[:, None]
    fwd_x = banded(taps_x, BX, EX, 1, -1).reshape(VIEWS_DEV * BX, EX)
    back_x = jnp.transpose(banded(near_x, BX, EX, 1, -1).reshape(VIEWS_DEV * BX, EX))
    back_x = jnp.concatenate([back_x, back_x], axis=1).astype(BF16)
    y_fwd = banded(taps_y, Y, Y, 1, HALF)
    y_back = banded(back_y, Y, Y, -1, HALF)
    z_fwd = banded(taps_z, Z, Z, -1, HALF)
    z_back = banded(taps_z, Z, Z, 1, HALF)
    return (
        (two_terms(fwd_x, 1), two_terms(y_fwd, 2), two_terms(z_fwd, 1)),
        (back_x, two_terms(y_back, 2), two_terms(z_back, 1)),
    )


def pack_kernel(me_ref, dest_ref, tiles_ref, *refs):
    outs, (order_ref, count_ref) = refs[:SPAN], refs[SPAN:]
    me = me_ref[0]
    for k in range(SPAN):
        count_ref[k] = 0
    for n in range(SLOTS):
        step = lax.rem(dest_ref[n, 0] - me + SPAN // 2 + 64, 64)
        rank = count_ref[step]
        count_ref[step] = rank + 1
        order_ref[step * CAP + rank] = n
    for k in range(SPAN):
        codes = []
        for c in range(CAP):
            n = order_ref[k * CAP + c]
            outs[k][c * TROWS : (c + 1) * TROWS, :] = tiles_ref[n]
            code = dest_ref[n, 1] * (BX // TP) + dest_ref[n, 2]
            codes.append(jnp.full((8, Z), code, jnp.int32).astype(F32))
        outs[k][CAP * TROWS :, :] = jnp.concatenate(codes, axis=0).astype(BF16)


def pack_tiles(view_tiles, tile_dest):
    me = lax.axis_index("block").astype(jnp.int32).reshape(1)
    return pl.pallas_call(
        pack_kernel,
        out_shape=[jax.ShapeDtypeStruct((PROWS, Z), BF16)] * SPAN,
        in_specs=[
            pl.BlockSpec(memory_space=pltpu.SMEM),
            pl.BlockSpec(memory_space=pltpu.SMEM),
            pl.BlockSpec(memory_space=pltpu.VMEM),
        ],
        out_specs=[pl.BlockSpec(memory_space=pltpu.VMEM)] * SPAN,
        scratch_shapes=[pltpu.SMEM((SLOTS,), jnp.int32), pltpu.SMEM((SPAN,), jnp.int32)],
        compiler_params=pltpu.CompilerParams(vmem_limit_bytes=VMEM_LIMIT),
        cost_estimate=pl.CostEstimate(flops=0, bytes_accessed=2 * SLOTS * TROWS * Z * 2, transcendentals=0),
        name="pack_tiles",
    )(me, tile_dest[0], view_tiles.reshape(SLOTS, TROWS, Z))


def level_of(peak):
    level = jnp.full(peak.shape, -LEVELS, F32)
    for j in range(-LEVELS, LEVELS):
        level = jnp.where(peak > 2.0 ** (14 + 16 * j), j + 1.0, level)
    return level


def scale_of(level):
    scale = jnp.ones(level.shape, F32)
    for j in range(-LEVELS, LEVELS + 1):
        if j:
            scale = jnp.where(level == j, 2.0 ** (16 * j), scale)
    return scale


def swapped(block):
    return jnp.transpose(block, (1, 0, 2))


def blur_into(kx_ref, ky_ref, kz_ref, parts, half_ref, out_ref):
    def along_x(t, carry):
        y0 = pl.multiple_of(t * SUB, SUB)
        data = jnp.concatenate([ref[:, pl.ds(y0, SUB), :] for ref in parts], axis=0).astype(F32)
        for h in range(0, SUB, 8):
            rows = swapped(data[:, h : h + 8]).astype(BF16)
            outs = []
            for j in range(0, 8, 2):
                pair = jnp.concatenate([rows[j], rows[j + 1]], axis=1)
                got = jnp.dot(
                    kx_ref[...], jnp.concatenate([pair, pair], axis=0), preferred_element_type=F32
                )
                outs += [got[:, :Z], got[:, Z:]]
            half_ref[:, pl.ds(y0 + h, 8), :] = swapped(jnp.stack(outs, axis=0))
        return carry

    lax.fori_loop(0, Y // SUB, along_x, 0)

    def along_yz(q, carry):
        v = q // (BX // TP)
        outs = []
        for i in range(0, TP, 2):
            pair = jnp.concatenate(
                [half_ref[q * TP + i + j].astype(BF16) for j in range(2)], axis=1
            )
            got = jnp.dot(
                ky_ref[v], jnp.concatenate([pair, pair], axis=0), preferred_element_type=F32
            ).astype(BF16)
            outs += [got[:, :Z], got[:, Z:]]
        rows = jnp.concatenate(outs, axis=0)
        out_ref[q] = jnp.dot(
            jnp.concatenate([rows, rows], axis=1), kz_ref[v], preferred_element_type=F32
        )
        return carry

    lax.fori_loop(0, VIEWS_DEV * BX // TP, along_yz, 0, unroll=UNROLL)


def back_from(kx_ref, ky_ref, kz_ref, measured_ref, blurred_ref, half_ref, edge_ref, outs):
    left_ref, mid_ref, right_ref = outs

    def along_zy(q, carry):
        v = q // (BX // TP)
        ratio = (measured_ref[q].astype(F32) / blurred_ref[q]).astype(BF16)
        rows = jnp.dot(
            jnp.concatenate([ratio, ratio], axis=1), kz_ref[v], preferred_element_type=F32
        ).astype(BF16)
        for i in range(0, TP, 2):
            pair = jnp.concatenate([rows[(i + j) * Y : (i + j + 1) * Y] for j in range(2)], axis=1)
            got = jnp.dot(
                ky_ref[v], jnp.concatenate([pair, pair], axis=0), preferred_element_type=F32
            )
            for j in range(2):
                half_ref[q * TP + i + j] = got[:, j * Z : (j + 1) * Z]
        return carry

    lax.fori_loop(0, VIEWS_DEV * BX // TP, along_zy, 0, unroll=UNROLL)

    def along_x(t, peak):
        y0 = pl.multiple_of(t * 8, 8)
        data = swapped(half_ref[:, pl.ds(y0, 8), :])
        high = data.astype(BF16)
        low = (data - high.astype(F32)).astype(BF16)
        got = []
        for j in range(0, 8, 2):
            pair = [jnp.concatenate([part[j], part[j + 1]], axis=1) for part in (high, low)]
            both = jnp.dot(
                kx_ref[...], jnp.concatenate(pair, axis=0), preferred_element_type=F32
            )
            got += [both[:, :Z], both[:, Z:]]
        planes = swapped(jnp.stack(got, axis=0))
        edge_ref[0, :, pl.ds(y0, 8), :] = planes[:HX]
        mid_ref[:, pl.ds(y0, 8), :] = planes[HX : HX + BX]
        edge_ref[1, :, pl.ds(y0, 8), :] = planes[HX + BX :]
        return jnp.maximum(peak, jnp.max(planes, axis=0))

    peak = lax.fori_loop(0, Y // 8, along_x, jnp.zeros((8, Z), F32), unroll=UNROLL)
    level = level_of(jnp.full((8, Z), jnp.max(peak), F32))
    shrink = scale_of(-level)[0:1]
    for i, ref in enumerate((left_ref, right_ref)):
        for p in range(HX):
            ref[p * Y : (p + 1) * Y, :] = edge_ref[i, p] * shrink
        ref[HX * Y :, :] = jnp.concatenate([level, level], axis=0)


def first_blur_kernel(kx_ref, ky_ref, kz_ref, left_ref, mid_ref, right_ref, out_ref, half_ref):
    blur_into(kx_ref, ky_ref, kz_ref, (left_ref, mid_ref, right_ref), half_ref, out_ref)


def first_back_kernel(kx_ref, ky_ref, kz_ref, blurred_ref, *refs):
    tiles = refs[:SPAN]
    left_ref, mid_ref, right_ref, measured_ref, half_ref, edge_ref = refs[SPAN:]
    for k in range(SPAN):
        for c in range(CAP):
            code = tiles[k][CAP * TROWS :, :].astype(F32)[8 * c, 0].astype(jnp.int32)
            measured_ref[code] = tiles[k][c * TROWS : (c + 1) * TROWS, :]
    outs = (left_ref, mid_ref, right_ref)
    back_from(kx_ref, ky_ref, kz_ref, measured_ref, blurred_ref, half_ref, edge_ref, outs)


def sweep_kernel(*refs):
    fwd, back, parts = refs[0:3], refs[3:6], refs[6:9]
    measured_ref = refs[9]
    outs = refs[10:13]
    half_ref, back_half_ref, edge_ref, blurred_ref = refs[13:]
    blur_into(*fwd, parts, half_ref, blurred_ref)
    back_from(*back, measured_ref, blurred_ref, back_half_ref, edge_ref, outs)


VM = pl.BlockSpec(memory_space=pltpu.VMEM)
BLURRED = (VIEWS_DEV * BX // TP, TROWS, Z)
HALF_SHAPE = (VIEWS_DEV * BX, Y, Z)
EDGE_ROWS = HX * Y + SUB
EDGE = jax.ShapeDtypeStruct((EDGE_ROWS, Z), F32)
CONTRIB = [EDGE, jax.ShapeDtypeStruct((BX, Y, Z), F32), EDGE]
EDGE_SCRATCH = pltpu.VMEM((2, HX, Y, Z), F32)


def call(kernel, name, operands, out_shape, scratch, flops):
    return pl.pallas_call(
        kernel,
        out_shape=out_shape,
        in_specs=[VM] * len(operands),
        out_specs=jax.tree.map(lambda _: VM, out_shape),
        scratch_shapes=scratch,
        compiler_params=pltpu.CompilerParams(vmem_limit_bytes=VMEM_LIMIT),
        cost_estimate=pl.CostEstimate(flops=flops, bytes_accessed=12 << 20, transcendentals=0),
        name=name,
    )(*operands)


def neighbours(low, high):
    size = lax.axis_size("block")
    up = [(i, i + 1) for i in range(size - 1)]
    down = [(j, i) for i, j in up]
    return lax.ppermute(high, "block", up), lax.ppermute(low, "block", down)


def with_halo(estimate):
    planes = estimate.astype(BF16)
    left, right = neighbours(planes[:HX], planes[HX:])
    return left, planes, right


def updated(estimate, contributions, view_count):
    left, mid, right = contributions
    arrived = neighbours(*lax.optimization_barrier((left.astype(F16), right.astype(F16))))
    level = left[HX * Y :]
    added = []
    for edge in arrived:
        edge_level = edge[HX * Y :].astype(F32)
        level = jnp.maximum(level, edge_level)
        added.append((edge[: HX * Y].reshape(HX, Y, Z).astype(F32), scale_of(edge_level)[0, 0]))
    scales, shrink, level = lax.optimization_barrier(
        ([scale for _, scale in added], scale_of(-level)[0, 0], level)
    )
    partial = mid + jnp.concatenate(
        [planes * scale for (planes, _), scale in zip(added, scales)], axis=0
    )
    own = lax.optimization_barrier((partial * shrink).astype(F16))
    swap = [(0, 1), (1, 0)]
    other, other_level = lax.ppermute((own, level), "view", swap)
    own_scale, other_scale = lax.optimization_barrier(
        (scale_of(level)[0, 0], scale_of(other_level)[0, 0])
    )
    total = own.astype(F32) * own_scale + other.astype(F32) * other_scale
    return estimate * total / view_count


def shards(estimate, view_tiles, tile_dest, psf_taps):
    kernels = psf_taps / jnp.sum(psf_taps, axis=-1, keepdims=True)
    view_count = kernels.shape[0] * lax.axis_size("view")
    blocks = lax.axis_size("block")
    packed = pack_tiles(view_tiles, tile_dest)
    arrived = []
    for k in range(SPAN):
        by = k - SPAN // 2
        perm = [(i, (i + by) % blocks) for i in range(blocks)]
        arrived.append(lax.ppermute(packed[k], "block", perm) if by else packed[k])
    fwd, back = blur_matrices(kernels)
    blurred = call(
        first_blur_kernel,
        "first_blur",
        (*fwd, *with_halo(estimate)),
        jax.ShapeDtypeStruct(BLURRED, F32),
        [pltpu.VMEM(HALF_SHAPE, F32)],
        6 << 30,
    )
    *contributions, measured = call(
        first_back_kernel,
        "first_back",
        (*back, blurred, *arrived),
        [*CONTRIB, jax.ShapeDtypeStruct((VIEWS_DEV * BX // TP, TROWS, Z), BF16)],
        [pltpu.VMEM(HALF_SHAPE, F32), EDGE_SCRATCH],
        8 << 30,
    )
    estimate = updated(estimate, contributions, view_count)
    contributions = call(
        sweep_kernel,
        "sweep",
        (*fwd, *back, *with_halo(estimate), measured),
        CONTRIB,
        [
            pltpu.VMEM(HALF_SHAPE, F32),
            pltpu.VMEM(HALF_SHAPE, F32),
            EDGE_SCRATCH,
            pltpu.VMEM(BLURRED, F32),
        ],
        14 << 30,
    )
    return updated(estimate, contributions, view_count)


def solution(mesh):
    return jax.shard_map(
        shards,
        mesh=mesh,
        in_specs=(
            P("block", None, None),
            P("view", "block", None, None, None),
            P("view", "block", None),
            P("view", None, None),
        ),
        out_specs=P("block", None, None),
        check_vma=False,
    )
```

```python
import functools

import jax
import jax.numpy as jnp
from jax import lax
from jax.experimental import pallas as pl
from jax.experimental.pallas import tpu as pltpu
from jax.sharding import PartitionSpec as P

TAPS = 31
HALF = TAPS // 2
BX = 32
HX = 16
EX = BX + 2 * HX
Y = 128
Z = 128
VIEWS_DEV = 3
ITERS = 2
CAP = 2
SPAN = 12
TP = 4
SLOTS = SPAN * CAP
TROWS = TP * Y
PROWS = CAP * TROWS + 16
SUB = 16
F32 = jnp.float32
BF16 = jnp.bfloat16
I16 = jnp.int16
VMEM_LIMIT = 56 << 20
UNROLL = 2


def banded(kernel, rows, cols, sign, offset):
    row_idx = jnp.arange(rows)[:, None]
    col_idx = jnp.arange(cols)[None, :]
    lag = sign * (col_idx - row_idx) + offset
    hits = (lag[:, :, None] == jnp.arange(kernel.shape[-1])[None, None, :]).astype(F32)
    return jnp.einsum("vt,ijt->vij", kernel, hits, precision=lax.Precision.HIGHEST)


def rounded(value):
    return lax.reduce_precision(value, 8, 7)


def two_terms(matrix, axis):
    high = rounded(matrix)
    return jnp.concatenate([high, matrix - high], axis=axis).astype(BF16)


def blur_matrices(kernels):
    taps_x, taps_y, taps_z = kernels[:, 0], kernels[:, 1], kernels[:, 2]
    near_x = rounded(taps_x)
    back_y = taps_y * (jnp.sum(taps_x, -1) / jnp.sum(near_x, -1))[:, None]
    fwd_x = banded(taps_x, BX, EX, 1, -1).reshape(VIEWS_DEV * BX, EX)
    back_x = jnp.transpose(banded(near_x, BX, EX, 1, -1).reshape(VIEWS_DEV * BX, EX))
    back_x = jnp.concatenate([back_x, back_x], axis=1).astype(BF16)
    y_fwd = banded(taps_y, Y, Y, 1, HALF)
    y_back = banded(back_y, Y, Y, -1, HALF)
    z_fwd = banded(taps_z, Z, Z, -1, HALF)
    z_back = banded(taps_z, Z, Z, 1, HALF)
    return (
        (two_terms(fwd_x, 1), two_terms(y_fwd, 2), two_terms(z_fwd, 1)),
        (back_x, two_terms(y_back, 2), two_terms(z_back, 1)),
    )


def pack_kernel(me_ref, dest_ref, tiles_ref, *refs):
    outs, (order_ref, count_ref) = refs[:SPAN], refs[SPAN:]
    me = me_ref[0]
    for k in range(SPAN):
        count_ref[k] = 0
    for n in range(SLOTS):
        step = lax.rem(dest_ref[n, 0] - me + SPAN // 2 + 64, 64)
        rank = count_ref[step]
        count_ref[step] = rank + 1
        order_ref[step * CAP + rank] = n
    for k in range(SPAN):
        codes = []
        for c in range(CAP):
            n = order_ref[k * CAP + c]
            outs[k][c * TROWS : (c + 1) * TROWS, :] = tiles_ref[n]
            code = dest_ref[n, 1] * (BX // TP) + dest_ref[n, 2]
            codes.append(jnp.full((8, Z), code, jnp.int32).astype(F32))
        outs[k][CAP * TROWS :, :] = jnp.concatenate(codes, axis=0).astype(BF16)


def pack_tiles(view_tiles, tile_dest):
    me = lax.axis_index("block").astype(jnp.int32).reshape(1)
    return pl.pallas_call(
        pack_kernel,
        out_shape=[jax.ShapeDtypeStruct((PROWS, Z), BF16)] * SPAN,
        in_specs=[
            pl.BlockSpec(memory_space=pltpu.SMEM),
            pl.BlockSpec(memory_space=pltpu.SMEM),
            pl.BlockSpec(memory_space=pltpu.VMEM),
        ],
        out_specs=[pl.BlockSpec(memory_space=pltpu.VMEM)] * SPAN,
        scratch_shapes=[pltpu.SMEM((SLOTS,), jnp.int32), pltpu.SMEM((SPAN,), jnp.int32)],
        compiler_params=pltpu.CompilerParams(vmem_limit_bytes=VMEM_LIMIT),
        cost_estimate=pl.CostEstimate(flops=0, bytes_accessed=2 * SLOTS * TROWS * Z * 2, transcendentals=0),
        name="pack_tiles",
    )(me, tile_dest[0], view_tiles.reshape(SLOTS, TROWS, Z))


STEPS = (64, 32, 16, 8, 4, 2, 1)
OFFSET = 64


def column_codes(peak):
    bound = peak * (2.0**-15 * (1 + 2.0**-12))
    scale = jnp.full(peak.shape, 2.0 ** (1 - OFFSET), F32)
    shrink = jnp.full(peak.shape, 2.0 ** (OFFSET - 1), F32)
    power = jnp.full(peak.shape, 1.0 - OFFSET, F32)
    for step in STEPS:
        larger = scale * 2.0 ** (step - 1) <= bound
        scale = jnp.where(larger, scale * 2.0**step, scale)
        shrink = jnp.where(larger, shrink * 2.0**-step, shrink)
        power = jnp.where(larger, power + step, power)
    return shrink, power


def column_scales(power):
    left = power + OFFSET
    scale = jnp.full(power.shape, 2.0**-OFFSET, F32)
    for step in STEPS:
        larger = left >= step
        scale = jnp.where(larger, scale * 2.0**step, scale)
        left = jnp.where(larger, left - step, left)
    return scale


def to_codes(values):
    return jnp.round(values).astype(jnp.int32).astype(I16)


def from_codes(codes):
    return codes.astype(jnp.int32).astype(F32)


def write_payload(ref, planes, peak):
    shrink, power = column_codes(peak)
    for p in range(HX):
        ref[p * Y : (p + 1) * Y, :] = to_codes(planes[p] * shrink[p : p + 1])
    ref[HX * Y :, :] = power.astype(jnp.int32).astype(I16)


def payload_scales(ref):
    return column_scales(from_codes(ref[HX * Y :, :]))


def payload_plane(ref, scales, p):
    return from_codes(ref[p * Y : (p + 1) * Y, :]) * scales[p : p + 1]


def swapped(block):
    return jnp.transpose(block, (1, 0, 2))


def blur_into(kx_ref, ky_ref, kz_ref, parts, half_ref, out_ref):
    def along_x(t, carry):
        y0 = pl.multiple_of(t * SUB, SUB)
        data = jnp.concatenate([ref[:, pl.ds(y0, SUB), :] for ref in parts], axis=0).astype(F32)
        for h in range(0, SUB, 8):
            rows = swapped(data[:, h : h + 8]).astype(BF16)
            outs = []
            for j in range(0, 8, 2):
                pair = jnp.concatenate([rows[j], rows[j + 1]], axis=1)
                got = jnp.dot(
                    kx_ref[...], jnp.concatenate([pair, pair], axis=0), preferred_element_type=F32
                )
                outs += [got[:, :Z], got[:, Z:]]
            half_ref[:, pl.ds(y0 + h, 8), :] = swapped(jnp.stack(outs, axis=0))
        return carry

    lax.fori_loop(0, Y // SUB, along_x, 0)

    def along_yz(q, carry):
        v = q // (BX // TP)
        outs = []
        for i in range(0, TP, 2):
            pair = jnp.concatenate(
                [half_ref[q * TP + i + j].astype(BF16) for j in range(2)], axis=1
            )
            got = jnp.dot(
                ky_ref[v], jnp.concatenate([pair, pair], axis=0), preferred_element_type=F32
            ).astype(BF16)
            outs += [got[:, :Z], got[:, Z:]]
        rows = jnp.concatenate(outs, axis=0)
        out_ref[q] = jnp.dot(
            jnp.concatenate([rows, rows], axis=1), kz_ref[v], preferred_element_type=F32
        )
        return carry

    lax.fori_loop(0, VIEWS_DEV * BX // TP, along_yz, 0, unroll=UNROLL)


def back_from(kx_ref, ky_ref, kz_ref, measured_ref, blurred_ref, half_ref, edge_ref, peak_ref, outs):
    left_ref, low_ref, high_ref, right_ref = outs

    def along_zy(q, carry):
        v = q // (BX // TP)
        ratio = (measured_ref[q].astype(F32) / blurred_ref[q]).astype(BF16)
        rows = jnp.dot(
            jnp.concatenate([ratio, ratio], axis=1), kz_ref[v], preferred_element_type=F32
        ).astype(BF16)
        for i in range(0, TP, 2):
            pair = jnp.concatenate([rows[(i + j) * Y : (i + j + 1) * Y] for j in range(2)], axis=1)
            got = jnp.dot(
                ky_ref[v], jnp.concatenate([pair, pair], axis=0), preferred_element_type=F32
            )
            for j in range(2):
                half_ref[q * TP + i + j] = got[:, j * Z : (j + 1) * Z]
        return carry

    lax.fori_loop(0, VIEWS_DEV * BX // TP, along_zy, 0, unroll=UNROLL)

    def along_x(t, carry):
        y0 = pl.multiple_of(t * 8, 8)
        data = swapped(half_ref[:, pl.ds(y0, 8), :])
        high = data.astype(BF16)
        low = (data - high.astype(F32)).astype(BF16)
        got = []
        for j in range(0, 8, 2):
            pair = [jnp.concatenate([part[j], part[j + 1]], axis=1) for part in (high, low)]
            both = jnp.dot(
                kx_ref[...], jnp.concatenate(pair, axis=0), preferred_element_type=F32
            )
            got += [both[:, :Z], both[:, Z:]]
        planes = swapped(jnp.stack(got, axis=0))
        for i, ref in enumerate((edge_ref.at[0], low_ref, high_ref, edge_ref.at[1])):
            ref[:, pl.ds(y0, 8), :] = planes[i * HX : (i + 1) * HX]
        for i, part in enumerate((planes[:HX], planes[HX + BX :])):
            peak_ref[i] = jnp.maximum(peak_ref[i], part)
        return carry

    peak_ref[...] = jnp.zeros(peak_ref.shape, F32)
    lax.fori_loop(0, Y // 8, along_x, 0, unroll=UNROLL)
    for i, ref in enumerate((left_ref, right_ref)):
        write_payload(ref, edge_ref.at[i], jnp.max(peak_ref[i], axis=1))


def first_blur_kernel(kx_ref, ky_ref, kz_ref, *refs):
    *parts, out_ref, half_ref = refs
    blur_into(kx_ref, ky_ref, kz_ref, parts, half_ref, out_ref)


def first_back_kernel(kx_ref, ky_ref, kz_ref, blurred_ref, *refs):
    tiles = refs[:SPAN]
    *outs, measured_ref, half_ref, edge_ref, peak_ref = refs[SPAN:]
    for k in range(SPAN):
        for c in range(CAP):
            code = tiles[k][CAP * TROWS :, :].astype(F32)[8 * c, 0].astype(jnp.int32)
            measured_ref[code] = tiles[k][c * TROWS : (c + 1) * TROWS, :]
    back_from(kx_ref, ky_ref, kz_ref, measured_ref, blurred_ref, half_ref, edge_ref, peak_ref, outs)


def sweep_kernel(*refs):
    fwd, back, parts = refs[0:3], refs[3:6], refs[6:10]
    measured_ref = refs[10]
    outs = refs[11:15]
    half_ref, back_half_ref, edge_ref, peak_ref, blurred_ref = refs[15:]
    blur_into(*fwd, parts, half_ref, blurred_ref)
    back_from(*back, measured_ref, blurred_ref, back_half_ref, edge_ref, peak_ref, outs)


def join_kernel(own_ref, edge_ref, out_ref, sum_ref):
    scales = payload_scales(edge_ref)
    peaks = []
    for p in range(HX):
        plane = own_ref[p] + payload_plane(edge_ref, scales, p)
        sum_ref[p] = plane
        peaks.append(jnp.max(plane, axis=0, keepdims=True))
    write_payload(out_ref, sum_ref, jnp.concatenate(peaks, axis=0))


def update_planes(view_count, before_ref, own_ref, other_ref, out_refs):
    own, other = payload_scales(own_ref), payload_scales(other_ref)
    for p in range(HX):
        total = payload_plane(own_ref, own, p) + payload_plane(other_ref, other, p)
        plane = before_ref[p] * total * (1.0 / view_count)
        for ref in out_refs:
            ref[p] = plane.astype(ref.dtype)


def update_kernel(view_count, before_ref, own_ref, other_ref, *out_refs):
    update_planes(view_count, before_ref, own_ref, other_ref, out_refs)


def last_kernel(view_count, low_ref, high_ref, *refs):
    *payloads, out_ref = refs
    for i, before_ref in enumerate((low_ref, high_ref)):
        own_ref, other_ref = payloads[2 * i : 2 * i + 2]
        update_planes(view_count, before_ref, own_ref, other_ref, (out_ref.at[pl.ds(i * HX, HX)],))


VM = pl.BlockSpec(memory_space=pltpu.VMEM)
BLURRED = (VIEWS_DEV * BX // TP, TROWS, Z)
HALF_SHAPE = (VIEWS_DEV * BX, Y, Z)
PAYLOAD = jax.ShapeDtypeStruct((HX * Y + HX, Z), I16)
OWN = jax.ShapeDtypeStruct((HX, Y, Z), F32)
CONTRIB = [PAYLOAD, OWN, OWN, PAYLOAD]
BLUR_SCRATCH = [pltpu.VMEM(HALF_SHAPE, F32)]
BACK_SCRATCH = [
    pltpu.VMEM(HALF_SHAPE, F32),
    pltpu.VMEM((2, HX, Y, Z), F32),
    pltpu.VMEM((2, HX, 8, Z), F32),
]


def call(kernel, name, operands, out_shape, scratch, flops):
    return pl.pallas_call(
        kernel,
        out_shape=out_shape,
        in_specs=[VM] * len(operands),
        out_specs=jax.tree.map(lambda _: VM, out_shape),
        scratch_shapes=scratch,
        compiler_params=pltpu.CompilerParams(vmem_limit_bytes=VMEM_LIMIT),
        cost_estimate=pl.CostEstimate(flops=flops, bytes_accessed=12 << 20, transcendentals=0),
        name=name,
    )(*operands)


def neighbours(low, high):
    size = lax.axis_size("block")
    up = [(i, i + 1) for i in range(size - 1)]
    down = [(j, i) for i, j in up]
    return lax.ppermute(high, "block", up), lax.ppermute(low, "block", down)


def exchanged(contributions):
    left, low, high, right = contributions
    pairs = []
    for own, edge in zip((low, high), neighbours(left, right)):
        payload = call(join_kernel, "join", (own, edge), PAYLOAD, [pltpu.VMEM(OWN.shape, F32)], 1 << 20)
        pairs.append((payload, lax.ppermute(payload, "view", [(0, 1), (1, 0)])))
    return pairs


def shards(estimate, view_tiles, tile_dest, psf_taps):
    kernels = psf_taps / jnp.sum(psf_taps, axis=-1, keepdims=True)
    view_count = kernels.shape[0] * lax.axis_size("view")
    blocks = lax.axis_size("block")
    packed = pack_tiles(view_tiles, tile_dest)
    arrived = []
    for k in range(SPAN):
        by = k - SPAN // 2
        perm = [(i, (i + by) % blocks) for i in range(blocks)]
        arrived.append(lax.ppermute(packed[k], "block", perm) if by else packed[k])
    fwd, back = blur_matrices(kernels)
    planes = estimate.astype(BF16)
    low, high = planes[:HX], planes[HX:]
    left, right = neighbours(low, high)
    blurred = call(
        first_blur_kernel,
        "first_blur",
        (*fwd, left, low, high, right),
        jax.ShapeDtypeStruct(BLURRED, F32),
        BLUR_SCRATCH,
        6 << 30,
    )
    *contributions, measured = call(
        first_back_kernel,
        "first_back",
        (*back, blurred, *arrived),
        [*CONTRIB, jax.ShapeDtypeStruct((VIEWS_DEV * BX // TP, TROWS, Z), BF16)],
        BACK_SCRATCH,
        8 << 30,
    )
    halves = []
    for i, (own, other) in enumerate(exchanged(contributions)):
        halves.append(
            call(
                functools.partial(update_kernel, view_count),
                "update",
                (estimate[i * HX : (i + 1) * HX], own, other),
                [OWN, jax.ShapeDtypeStruct(OWN.shape, BF16)],
                [],
                1 << 20,
            )
        )
    (low, low_planes), (high, high_planes) = halves
    left, right = neighbours(low_planes, high_planes)
    contributions = call(
        sweep_kernel,
        "sweep",
        (*fwd, *back, left, low_planes, high_planes, right, measured),
        CONTRIB,
        [*BLUR_SCRATCH, *BACK_SCRATCH, pltpu.VMEM(BLURRED, F32)],
        14 << 30,
    )
    payloads = [payload for pair in exchanged(contributions) for payload in pair]
    return call(
        functools.partial(last_kernel, view_count),
        "last_update",
        (low, high, *payloads),
        jax.ShapeDtypeStruct(estimate.shape, F32),
        [],
        1 << 20,
    )


def solution(mesh):
    return jax.shard_map(
        shards,
        mesh=mesh,
        in_specs=(
            P("block", None, None),
            P("view", "block", None, None, None),
            P("view", "block", None),
            P("view", None, None),
        ),
        out_specs=P("block", None, None),
        check_vma=False,
    )
```

```python
import functools

import jax
import jax.numpy as jnp
from jax import lax
from jax.experimental import pallas as pl
from jax.experimental.pallas import tpu as pltpu
from jax.sharding import PartitionSpec as P

TAPS = 31
HALF = TAPS // 2
BX = 32
HX = 16
EX = BX + 2 * HX
Y = 128
Z = 128
LANES = 128
VIEWS_DEV = 3
ITERS = 2
CAP = 2
SPAN = 12
TP = 4
SLOTS = SPAN * CAP
TROWS = TP * Y
PROWS = CAP * TROWS + 16
SUB = 16
F32 = jnp.float32
BF16 = jnp.bfloat16
I16 = jnp.int16
VMEM_LIMIT = 56 << 20
UNROLL = 4
EARLY = (-6, 5, -5, 4, -4, 3, -3)
LATE = (2, -2, 1, -1)


def toeplitz(row, rows, shift, low, high):
    turned = pltpu.roll(
        jnp.broadcast_to(row, (rows, LANES)), shift % LANES, 1, stride=1, stride_axis=0
    )
    lag = lax.broadcasted_iota(jnp.int32, (rows, LANES), 1) - lax.broadcasted_iota(
        jnp.int32, (rows, LANES), 0
    )
    return jnp.where((lag >= low) & (lag <= high), turned, 0.0)


def prepare_kernel(psf_ref, *refs):
    *outs, taps_ref, turned_ref = refs
    fwd_x_ref, fwd_y_ref, fwd_z_ref, back_x_ref, back_y_ref, back_z_ref = outs
    dims = psf_ref.shape[1]
    taps_ref[...] = jnp.zeros(taps_ref.shape, F32)
    for v in range(VIEWS_DEV):
        taps = psf_ref[v]
        taps_ref[v * dims : (v + 1) * dims, :TAPS] = taps / jnp.sum(taps, axis=1, keepdims=True)
    turned_ref[...] = jnp.transpose(taps_ref[...])
    left_over = jnp.zeros((1, LANES), F32)
    for a in range(TAPS):
        wanted = turned_ref[a : a + 1, :] + left_over
        near = wanted.astype(BF16).astype(F32)
        left_over = wanted - near
        turned_ref[a : a + 1, :] = near
    taps_ref[...] = jnp.transpose(turned_ref[...])
    for a in range(TAPS):
        turned_ref[TAPS + 1 + a : TAPS + 2 + a, :] = turned_ref[TAPS - 1 - a : TAPS - a, :]
    turned_ref[:TAPS, :] = turned_ref[TAPS + 1 : 2 * TAPS + 1, :]
    turned_ref[TAPS:, :] = jnp.zeros((LANES - TAPS, LANES), F32)
    turned_ref[...] = jnp.transpose(turned_ref[...])
    wide = []
    for v in range(VIEWS_DEV):
        ahead = [taps_ref[v * dims + d : v * dims + d + 1, :] for d in range(dims)]
        behind = [turned_ref[v * dims + d : v * dims + d + 1, :] for d in range(dims)]
        wide.append(toeplitz(ahead[0], BX, 1, 1, TAPS))
        for ref, row in (
            (fwd_y_ref, ahead[1]),
            (back_y_ref, behind[1]),
            (fwd_z_ref, behind[2]),
            (back_z_ref, ahead[2]),
        ):
            ref[v] = toeplitz(row, LANES, -HALF, -HALF, HALF).astype(BF16)
    along = jnp.concatenate(wide, axis=0)
    fwd_x_ref[...] = along[:, :EX].astype(BF16)
    full = jnp.concatenate([along, jnp.zeros((LANES - VIEWS_DEV * BX, LANES), F32)], axis=0)
    across = jnp.transpose(full)[:EX, : VIEWS_DEV * BX].astype(BF16)
    back_x_ref[...] = jnp.concatenate([across, across], axis=1)


def blur_matrices(psf_taps):
    square = jax.ShapeDtypeStruct((VIEWS_DEV, LANES, LANES), BF16)
    shapes = [
        jax.ShapeDtypeStruct((VIEWS_DEV * BX, EX), BF16),
        square,
        square,
        jax.ShapeDtypeStruct((EX, 2 * VIEWS_DEV * BX), BF16),
        square,
        square,
    ]
    scratch = [pltpu.VMEM((LANES, LANES), F32)] * 2
    matrices = call(prepare_kernel, "prepare", (psf_taps,), shapes, scratch, 1 << 20)
    return matrices[:3], matrices[3:]


def pack_kernel(me_ref, dest_ref, tiles_ref, *refs):
    outs, (order_ref, count_ref) = refs[:SPAN], refs[SPAN:]
    me = me_ref[0]
    for k in range(SPAN):
        count_ref[k] = 0
    for n in range(SLOTS):
        step = lax.rem(dest_ref[n, 0] - me + SPAN // 2 + 64, 64)
        rank = count_ref[step]
        count_ref[step] = rank + 1
        order_ref[step * CAP + rank] = n
    for k in range(SPAN):
        codes = []
        for c in range(CAP):
            n = order_ref[k * CAP + c]
            outs[k][c * TROWS : (c + 1) * TROWS, :] = tiles_ref[n]
            code = dest_ref[n, 1] * (BX // TP) + dest_ref[n, 2]
            codes.append(jnp.full((8, Z), code, jnp.int32).astype(F32))
        outs[k][CAP * TROWS :, :] = jnp.concatenate(codes, axis=0).astype(BF16)


def pack_tiles(view_tiles, tile_dest):
    me = lax.axis_index("block").astype(jnp.int32).reshape(1)
    return pl.pallas_call(
        pack_kernel,
        out_shape=[jax.ShapeDtypeStruct((PROWS, Z), BF16)] * SPAN,
        in_specs=[
            pl.BlockSpec(memory_space=pltpu.SMEM),
            pl.BlockSpec(memory_space=pltpu.SMEM),
            pl.BlockSpec(memory_space=pltpu.VMEM),
        ],
        out_specs=[pl.BlockSpec(memory_space=pltpu.VMEM)] * SPAN,
        scratch_shapes=[pltpu.SMEM((SLOTS,), jnp.int32), pltpu.SMEM((SPAN,), jnp.int32)],
        compiler_params=pltpu.CompilerParams(vmem_limit_bytes=VMEM_LIMIT),
        cost_estimate=pl.CostEstimate(flops=0, bytes_accessed=2 * SLOTS * TROWS * Z * 2, transcendentals=0),
        name="pack_tiles",
    )(me, tile_dest[0], view_tiles.reshape(SLOTS, TROWS, Z))


STEPS = (64, 32, 16, 8, 4, 2, 1)
OFFSET = 64


def column_codes(peak):
    bound = peak * (2.0**-15 * (1 + 2.0**-12))
    scale = jnp.full(peak.shape, 2.0 ** (1 - OFFSET), F32)
    shrink = jnp.full(peak.shape, 2.0 ** (OFFSET - 1), F32)
    power = jnp.full(peak.shape, 1.0 - OFFSET, F32)
    for step in STEPS:
        larger = scale * 2.0 ** (step - 1) <= bound
        scale = jnp.where(larger, scale * 2.0**step, scale)
        shrink = jnp.where(larger, shrink * 2.0**-step, shrink)
        power = jnp.where(larger, power + step, power)
    return shrink, power


def column_scales(power):
    left = power + OFFSET
    scale = jnp.full(power.shape, 2.0**-OFFSET, F32)
    for step in STEPS:
        larger = left >= step
        scale = jnp.where(larger, scale * 2.0**step, scale)
        left = jnp.where(larger, left - step, left)
    return scale


def to_codes(values):
    return jnp.round(values).astype(jnp.int32).astype(I16)


def from_codes(codes):
    return codes.astype(jnp.int32).astype(F32)


def write_payload(ref, planes, peak):
    shrink, power = column_codes(peak)
    for p in range(HX):
        ref[p * Y : (p + 1) * Y, :] = to_codes(planes[p] * shrink[p : p + 1])
    ref[HX * Y :, :] = power.astype(jnp.int32).astype(I16)


def payload_scales(ref):
    return column_scales(from_codes(ref[HX * Y :, :]))


def payload_plane(ref, scales, p):
    return from_codes(ref[p * Y : (p + 1) * Y, :]) * scales[p : p + 1]


def swapped(block):
    return jnp.transpose(block, (1, 0, 2))


def blur_into(kx_ref, ky_ref, kz_ref, parts, half_ref, out_ref):
    def along_x(t, carry):
        y0 = pl.multiple_of(t * SUB, SUB)
        data = jnp.concatenate([ref[:, pl.ds(y0, SUB), :] for ref in parts], axis=0).astype(F32)
        for h in range(0, SUB, 8):
            rows = swapped(data[:, h : h + 8]).astype(BF16)
            outs = []
            for j in range(0, 8, 2):
                pair = jnp.concatenate([rows[j], rows[j + 1]], axis=1)
                got = jnp.dot(kx_ref[...], pair, preferred_element_type=F32)
                outs += [got[:, :Z], got[:, Z:]]
            half_ref[:, pl.ds(y0 + h, 8), :] = swapped(jnp.stack(outs, axis=0))
        return carry

    lax.fori_loop(0, Y // SUB, along_x, 0, unroll=2)

    def along_yz(q, carry):
        v = q // (BX // TP)
        outs = []
        for i in range(0, TP, 2):
            pair = jnp.concatenate(
                [half_ref[q * TP + i + j].astype(BF16) for j in range(2)], axis=1
            )
            got = jnp.dot(ky_ref[v], pair, preferred_element_type=F32).astype(BF16)
            outs += [got[:, :Z], got[:, Z:]]
        rows = jnp.concatenate(outs, axis=0)
        out_ref[q] = jnp.dot(rows, kz_ref[v], preferred_element_type=F32)
        return carry

    lax.fori_loop(0, VIEWS_DEV * BX // TP, along_yz, 0, unroll=UNROLL)


def back_from(kx_ref, ky_ref, kz_ref, measured_ref, blurred_ref, half_ref, edge_ref, peak_ref, outs):
    left_ref, low_ref, high_ref, right_ref = outs

    def along_zy(q, carry):
        v = q // (BX // TP)
        ratio = (measured_ref[q].astype(F32) / blurred_ref[q]).astype(BF16)
        rows = jnp.dot(ratio, kz_ref[v], preferred_element_type=F32).astype(BF16)
        for i in range(0, TP, 2):
            pair = jnp.concatenate([rows[(i + j) * Y : (i + j + 1) * Y] for j in range(2)], axis=1)
            got = jnp.dot(ky_ref[v], pair, preferred_element_type=F32)
            for j in range(2):
                half_ref[q * TP + i + j] = got[:, j * Z : (j + 1) * Z]
        return carry

    lax.fori_loop(0, VIEWS_DEV * BX // TP, along_zy, 0, unroll=UNROLL)

    def along_x(t, carry):
        y0 = pl.multiple_of(t * 8, 8)
        data = swapped(half_ref[:, pl.ds(y0, 8), :])
        high = data.astype(BF16)
        low = (data - high.astype(F32)).astype(BF16)
        got = []
        for j in range(0, 8, 2):
            pair = [jnp.concatenate([part[j], part[j + 1]], axis=1) for part in (high, low)]
            both = jnp.dot(
                kx_ref[...], jnp.concatenate(pair, axis=0), preferred_element_type=F32
            )
            got += [both[:, :Z], both[:, Z:]]
        planes = swapped(jnp.stack(got, axis=0))
        for i, ref in enumerate((edge_ref.at[0], low_ref, high_ref, edge_ref.at[1])):
            ref[:, pl.ds(y0, 8), :] = planes[i * HX : (i + 1) * HX]
        for i, part in enumerate((planes[:HX], planes[HX + BX :])):
            peak_ref[i] = jnp.maximum(peak_ref[i], part)
        return carry

    peak_ref[...] = jnp.zeros(peak_ref.shape, F32)
    lax.fori_loop(0, Y // 8, along_x, 0, unroll=UNROLL)
    for i, ref in enumerate((left_ref, right_ref)):
        write_payload(ref, edge_ref.at[i], jnp.max(peak_ref[i], axis=1))


def first_blur_kernel(kx_ref, ky_ref, kz_ref, *refs):
    *parts, out_ref, half_ref = refs
    blur_into(kx_ref, ky_ref, kz_ref, parts, half_ref, out_ref)


def first_back_kernel(kx_ref, ky_ref, kz_ref, blurred_ref, *refs):
    tiles = refs[:SPAN]
    *outs, measured_ref, half_ref, edge_ref, peak_ref = refs[SPAN:]
    for k in range(SPAN):
        for c in range(CAP):
            code = tiles[k][CAP * TROWS :, :].astype(F32)[8 * c, 0].astype(jnp.int32)
            measured_ref[code] = tiles[k][c * TROWS : (c + 1) * TROWS, :]
    back_from(kx_ref, ky_ref, kz_ref, measured_ref, blurred_ref, half_ref, edge_ref, peak_ref, outs)


def sweep_kernel(*refs):
    fwd, back, parts = refs[0:3], refs[3:6], refs[6:10]
    measured_ref = refs[10]
    outs = refs[11:15]
    half_ref, back_half_ref, edge_ref, peak_ref, blurred_ref = refs[15:]
    blur_into(*fwd, parts, half_ref, blurred_ref)
    back_from(*back, measured_ref, blurred_ref, back_half_ref, edge_ref, peak_ref, outs)


def join_kernel(own_ref, edge_ref, out_ref, sum_ref):
    scales = payload_scales(edge_ref)
    peaks = []
    for p in range(HX):
        plane = own_ref[p] + payload_plane(edge_ref, scales, p)
        sum_ref[p] = plane
        peaks.append(jnp.max(plane, axis=0, keepdims=True))
    write_payload(out_ref, sum_ref, jnp.concatenate(peaks, axis=0))


def update_planes(view_count, before_ref, own_ref, other_ref, out_refs):
    own, other = payload_scales(own_ref), payload_scales(other_ref)
    for p in range(HX):
        total = payload_plane(own_ref, own, p) + payload_plane(other_ref, other, p)
        plane = before_ref[p] * total * (1.0 / view_count)
        for ref in out_refs:
            ref[p] = plane.astype(ref.dtype)


def update_kernel(view_count, before_ref, own_ref, other_ref, *out_refs):
    update_planes(view_count, before_ref, own_ref, other_ref, out_refs)


def last_kernel(view_count, low_ref, high_ref, *refs):
    *payloads, out_ref = refs
    for i, before_ref in enumerate((low_ref, high_ref)):
        own_ref, other_ref = payloads[2 * i : 2 * i + 2]
        update_planes(view_count, before_ref, own_ref, other_ref, (out_ref.at[pl.ds(i * HX, HX)],))


VM = pl.BlockSpec(memory_space=pltpu.VMEM)
BLURRED = (VIEWS_DEV * BX // TP, TROWS, Z)
HALF_SHAPE = (VIEWS_DEV * BX, Y, Z)
PAYLOAD = jax.ShapeDtypeStruct((HX * Y + HX, Z), I16)
OWN = jax.ShapeDtypeStruct((HX, Y, Z), F32)
CONTRIB = [PAYLOAD, OWN, OWN, PAYLOAD]
BLUR_SCRATCH = [pltpu.VMEM(HALF_SHAPE, F32)]
BACK_SCRATCH = [
    pltpu.VMEM(HALF_SHAPE, F32),
    pltpu.VMEM((2, HX, Y, Z), F32),
    pltpu.VMEM((2, HX, 8, Z), F32),
]


def call(kernel, name, operands, out_shape, scratch, flops):
    return pl.pallas_call(
        kernel,
        out_shape=out_shape,
        in_specs=[VM] * len(operands),
        out_specs=jax.tree.map(lambda _: VM, out_shape),
        scratch_shapes=scratch,
        compiler_params=pltpu.CompilerParams(vmem_limit_bytes=VMEM_LIMIT),
        cost_estimate=pl.CostEstimate(flops=flops, bytes_accessed=12 << 20, transcendentals=0),
        name=name,
    )(*operands)


def neighbours(low, high):
    size = lax.axis_size("block")
    up = [(i, i + 1) for i in range(size - 1)]
    down = [(j, i) for i, j in up]
    return lax.ppermute(high, "block", up), lax.ppermute(low, "block", down)


def exchanged(contributions):
    left, low, high, right = contributions
    pairs = []
    for own, edge in zip((low, high), neighbours(left, right)):
        payload = call(join_kernel, "join", (own, edge), PAYLOAD, [pltpu.VMEM(OWN.shape, F32)], 1 << 20)
        pairs.append((payload, lax.ppermute(payload, "view", [(0, 1), (1, 0)])))
    return pairs


def shards(estimate, view_tiles, tile_dest, psf_taps):
    view_count = psf_taps.shape[0] * lax.axis_size("view")
    blocks = lax.axis_size("block")
    packed = pack_tiles(view_tiles, tile_dest)
    estimate, psf_taps, packed = lax.optimization_barrier((estimate, psf_taps, packed))
    arrived = list(packed)

    def route(steps):
        for by in steps:
            perm = [(i, (i + by) % blocks) for i in range(blocks)]
            arrived[by + SPAN // 2] = lax.ppermute(packed[by + SPAN // 2], "block", perm)

    planes = estimate.astype(BF16)
    low, high = planes[:HX], planes[HX:]
    left, right = neighbours(low, high)
    route(EARLY)
    fwd, back = blur_matrices(psf_taps)
    blurred = call(
        first_blur_kernel,
        "first_blur",
        (*fwd, left, low, high, right),
        jax.ShapeDtypeStruct(BLURRED, F32),
        BLUR_SCRATCH,
        6 << 30,
    )
    packed, blurred = lax.optimization_barrier((packed, blurred))
    route(LATE)
    *contributions, measured = call(
        first_back_kernel,
        "first_back",
        (*back, blurred, *arrived),
        [*CONTRIB, jax.ShapeDtypeStruct((VIEWS_DEV * BX // TP, TROWS, Z), BF16)],
        BACK_SCRATCH,
        8 << 30,
    )
    halves = []
    for i, (own, other) in enumerate(exchanged(contributions)):
        halves.append(
            call(
                functools.partial(update_kernel, view_count),
                "update",
                (estimate[i * HX : (i + 1) * HX], own, other),
                [OWN, jax.ShapeDtypeStruct(OWN.shape, BF16)],
                [],
                1 << 20,
            )
        )
    (low, low_planes), (high, high_planes) = halves
    left, right = neighbours(low_planes, high_planes)
    contributions = call(
        sweep_kernel,
        "sweep",
        (*fwd, *back, left, low_planes, high_planes, right, measured),
        CONTRIB,
        [*BLUR_SCRATCH, *BACK_SCRATCH, pltpu.VMEM(BLURRED, F32)],
        14 << 30,
    )
    payloads = [payload for pair in exchanged(contributions) for payload in pair]
    return call(
        functools.partial(last_kernel, view_count),
        "last_update",
        (low, high, *payloads),
        jax.ShapeDtypeStruct(estimate.shape, F32),
        [],
        1 << 20,
    )


def solution(mesh):
    return jax.shard_map(
        shards,
        mesh=mesh,
        in_specs=(
            P("block", None, None),
            P("view", "block", None, None, None),
            P("view", "block", None),
            P("view", None, None),
        ),
        out_specs=P("block", None, None),
        check_vma=False,
    )
```

```python
import functools

import jax
import jax.numpy as jnp
from jax import lax
from jax.experimental import pallas as pl
from jax.experimental.pallas import tpu as pltpu
from jax.sharding import PartitionSpec as P

TAPS = 31
HALF = TAPS // 2
BX = 32
HX = 16
EX = BX + 2 * HX
Y = 128
Z = 128
LANES = 128
VIEWS_DEV = 3
ITERS = 2
CAP = 2
SPAN = 12
TP = 4
SLOTS = SPAN * CAP
TROWS = TP * Y
PROWS = CAP * TROWS + 16
SUB = 16
F32 = jnp.float32
BF16 = jnp.bfloat16
I16 = jnp.int16
MIB = 1 << 20
UNROLL = 4
EARLY = (-6, 5, -5, 4, -4, 3, -3)
LATE = (2, -2, 1, -1)


def toeplitz(row, rows, shift, low, high):
    turned = pltpu.roll(
        jnp.broadcast_to(row, (rows, LANES)), shift % LANES, 1, stride=1, stride_axis=0
    )
    lag = lax.broadcasted_iota(jnp.int32, (rows, LANES), 1) - lax.broadcasted_iota(
        jnp.int32, (rows, LANES), 0
    )
    return jnp.where((lag >= low) & (lag <= high), turned, 0.0)


def prepare_kernel(psf_ref, *refs):
    *outs, taps_ref, turned_ref = refs
    fwd_x_ref, fwd_y_ref, fwd_z_ref, back_x_ref, back_y_ref, back_z_ref = outs
    dims = psf_ref.shape[1]
    taps_ref[...] = jnp.zeros(taps_ref.shape, F32)
    for v in range(VIEWS_DEV):
        taps = psf_ref[v]
        taps_ref[v * dims : (v + 1) * dims, :TAPS] = taps / jnp.sum(taps, axis=1, keepdims=True)
    turned_ref[...] = jnp.transpose(taps_ref[...])
    left_over = jnp.zeros((1, LANES), F32)
    for a in range(TAPS):
        wanted = turned_ref[a : a + 1, :] + left_over
        near = wanted.astype(BF16).astype(F32)
        left_over = wanted - near
        turned_ref[a : a + 1, :] = near
    taps_ref[...] = jnp.transpose(turned_ref[...])
    for a in range(TAPS):
        turned_ref[TAPS + 1 + a : TAPS + 2 + a, :] = turned_ref[TAPS - 1 - a : TAPS - a, :]
    turned_ref[:TAPS, :] = turned_ref[TAPS + 1 : 2 * TAPS + 1, :]
    turned_ref[TAPS:, :] = jnp.zeros((LANES - TAPS, LANES), F32)
    turned_ref[...] = jnp.transpose(turned_ref[...])
    wide = []
    for v in range(VIEWS_DEV):
        ahead = [taps_ref[v * dims + d : v * dims + d + 1, :] for d in range(dims)]
        behind = [turned_ref[v * dims + d : v * dims + d + 1, :] for d in range(dims)]
        wide.append(toeplitz(ahead[0], BX, 1, 1, TAPS))
        for ref, row in (
            (fwd_y_ref, ahead[1]),
            (back_y_ref, behind[1]),
            (fwd_z_ref, behind[2]),
            (back_z_ref, ahead[2]),
        ):
            ref[v] = toeplitz(row, LANES, -HALF, -HALF, HALF).astype(BF16)
    along = jnp.concatenate(wide, axis=0)
    fwd_x_ref[...] = along[:, :EX].astype(BF16)
    full = jnp.concatenate([along, jnp.zeros((LANES - VIEWS_DEV * BX, LANES), F32)], axis=0)
    across = jnp.transpose(full)[:EX, : VIEWS_DEV * BX].astype(BF16)
    back_x_ref[...] = jnp.concatenate([across, across], axis=1)


def blur_matrices(psf_taps):
    square = jax.ShapeDtypeStruct((VIEWS_DEV, LANES, LANES), BF16)
    shapes = [
        jax.ShapeDtypeStruct((VIEWS_DEV * BX, EX), BF16),
        square,
        square,
        jax.ShapeDtypeStruct((EX, 2 * VIEWS_DEV * BX), BF16),
        square,
        square,
    ]
    scratch = [pltpu.VMEM((LANES, LANES), F32)] * 2
    matrices = call(prepare_kernel, "prepare", (psf_taps,), shapes, scratch, 1 << 20)
    return matrices[:3], matrices[3:]


def pack_kernel(me_ref, dest_ref, tiles_ref, *refs):
    outs, (order_ref, count_ref) = refs[:SPAN], refs[SPAN:]
    me = me_ref[0]
    for k in range(SPAN):
        count_ref[k] = 0
    for n in range(SLOTS):
        step = lax.rem(dest_ref[n, 0] - me + SPAN // 2 + 64, 64)
        rank = count_ref[step]
        count_ref[step] = rank + 1
        order_ref[step * CAP + rank] = n
    for k in range(SPAN):
        codes = []
        for c in range(CAP):
            n = order_ref[k * CAP + c]
            outs[k][c * TROWS : (c + 1) * TROWS, :] = tiles_ref[n]
            code = dest_ref[n, 1] * (BX // TP) + dest_ref[n, 2]
            codes.append(jnp.full((8, Z), code, jnp.int32).astype(F32))
        outs[k][CAP * TROWS :, :] = jnp.concatenate(codes, axis=0).astype(BF16)


def pack_tiles(view_tiles, tile_dest):
    me = lax.axis_index("block").astype(jnp.int32).reshape(1)
    return pl.pallas_call(
        pack_kernel,
        out_shape=[jax.ShapeDtypeStruct((PROWS, Z), BF16)] * SPAN,
        in_specs=[
            pl.BlockSpec(memory_space=pltpu.SMEM),
            pl.BlockSpec(memory_space=pltpu.SMEM),
            pl.BlockSpec(memory_space=pltpu.VMEM),
        ],
        out_specs=[pl.BlockSpec(memory_space=pltpu.VMEM)] * SPAN,
        scratch_shapes=[pltpu.SMEM((SLOTS,), jnp.int32), pltpu.SMEM((SPAN,), jnp.int32)],
        compiler_params=pltpu.CompilerParams(vmem_limit_bytes=8 * MIB),
        cost_estimate=pl.CostEstimate(flops=0, bytes_accessed=2 * SLOTS * TROWS * Z * 2, transcendentals=0),
        name="pack_tiles",
    )(me, tile_dest[0], view_tiles.reshape(SLOTS, TROWS, Z))


STEPS = (64, 32, 16, 8, 4, 2, 1)
OFFSET = 64


def column_codes(peak):
    bound = peak * (2.0**-15 * (1 + 2.0**-12))
    scale = jnp.full(peak.shape, 2.0 ** (1 - OFFSET), F32)
    shrink = jnp.full(peak.shape, 2.0 ** (OFFSET - 1), F32)
    power = jnp.full(peak.shape, 1.0 - OFFSET, F32)
    for step in STEPS:
        larger = scale * 2.0 ** (step - 1) <= bound
        scale = jnp.where(larger, scale * 2.0**step, scale)
        shrink = jnp.where(larger, shrink * 2.0**-step, shrink)
        power = jnp.where(larger, power + step, power)
    return shrink, power


def column_scales(power):
    left = power + OFFSET
    scale = jnp.full(power.shape, 2.0**-OFFSET, F32)
    for step in STEPS:
        larger = left >= step
        scale = jnp.where(larger, scale * 2.0**step, scale)
        left = jnp.where(larger, left - step, left)
    return scale


def to_codes(values):
    return jnp.round(values).astype(jnp.int32).astype(I16)


def from_codes(codes):
    return codes.astype(jnp.int32).astype(F32)


def write_payload(ref, planes, peak):
    shrink, power = column_codes(peak)
    for p in range(HX):
        ref[p * Y : (p + 1) * Y, :] = to_codes(planes[p] * shrink[p : p + 1])
    ref[HX * Y :, :] = power.astype(jnp.int32).astype(I16)


def payload_scales(ref):
    return column_scales(from_codes(ref[HX * Y :, :]))


def payload_plane(ref, scales, p):
    return from_codes(ref[p * Y : (p + 1) * Y, :]) * scales[p : p + 1]


def swapped(block):
    return jnp.transpose(block, (1, 0, 2))


def blur_into(kx_ref, ky_ref, kz_ref, parts, half_ref, out_ref):
    def along_x(t, carry):
        y0 = pl.multiple_of(t * SUB, SUB)
        data = jnp.concatenate([ref[:, pl.ds(y0, SUB), :] for ref in parts], axis=0).astype(F32)
        for h in range(0, SUB, 8):
            rows = swapped(data[:, h : h + 8]).astype(BF16)
            outs = []
            for j in range(0, 8, 2):
                pair = jnp.concatenate([rows[j], rows[j + 1]], axis=1)
                got = jnp.dot(kx_ref[...], pair, preferred_element_type=F32)
                outs += [got[:, :Z], got[:, Z:]]
            half_ref[:, pl.ds(y0 + h, 8), :] = swapped(jnp.stack(outs, axis=0))
        return carry

    lax.fori_loop(0, Y // SUB, along_x, 0, unroll=2)

    def along_yz(q, carry):
        v = q // (BX // TP)
        outs = []
        for i in range(0, TP, 2):
            pair = jnp.concatenate(
                [half_ref[q * TP + i + j].astype(BF16) for j in range(2)], axis=1
            )
            got = jnp.dot(ky_ref[v], pair, preferred_element_type=F32).astype(BF16)
            outs += [got[:, :Z], got[:, Z:]]
        rows = jnp.concatenate(outs, axis=0)
        out_ref[q] = jnp.dot(rows, kz_ref[v], preferred_element_type=F32)
        return carry

    lax.fori_loop(0, VIEWS_DEV * BX // TP, along_yz, 0, unroll=UNROLL)


def back_from(kx_ref, ky_ref, kz_ref, measured_ref, blurred_ref, half_ref, edge_ref, peak_ref, outs):
    left_ref, low_ref, high_ref, right_ref = outs

    def along_zy(q, carry):
        v = q // (BX // TP)
        ratio = (measured_ref[q].astype(F32) / blurred_ref[q]).astype(BF16)
        rows = jnp.dot(ratio, kz_ref[v], preferred_element_type=F32).astype(BF16)
        for i in range(0, TP, 2):
            pair = jnp.concatenate([rows[(i + j) * Y : (i + j + 1) * Y] for j in range(2)], axis=1)
            got = jnp.dot(ky_ref[v], pair, preferred_element_type=F32)
            for j in range(2):
                half_ref[q * TP + i + j] = got[:, j * Z : (j + 1) * Z]
        return carry

    lax.fori_loop(0, VIEWS_DEV * BX // TP, along_zy, 0, unroll=UNROLL)

    def along_x(t, carry):
        y0 = pl.multiple_of(t * 8, 8)
        data = swapped(half_ref[:, pl.ds(y0, 8), :])
        high = data.astype(BF16)
        low = (data - high.astype(F32)).astype(BF16)
        got = []
        for j in range(0, 8, 2):
            pair = [jnp.concatenate([part[j], part[j + 1]], axis=1) for part in (high, low)]
            both = jnp.dot(
                kx_ref[...], jnp.concatenate(pair, axis=0), preferred_element_type=F32
            )
            got += [both[:, :Z], both[:, Z:]]
        planes = swapped(jnp.stack(got, axis=0))
        for i, ref in enumerate((edge_ref.at[0], low_ref, high_ref, edge_ref.at[1])):
            ref[:, pl.ds(y0, 8), :] = planes[i * HX : (i + 1) * HX]
        for i, part in enumerate((planes[:HX], planes[HX + BX :])):
            peak_ref[i] = jnp.maximum(peak_ref[i], part)
        return carry

    peak_ref[...] = jnp.zeros(peak_ref.shape, F32)
    lax.fori_loop(0, Y // 8, along_x, 0, unroll=UNROLL)
    for i, ref in enumerate((left_ref, right_ref)):
        write_payload(ref, edge_ref.at[i], jnp.max(peak_ref[i], axis=1))


def first_blur_kernel(kx_ref, ky_ref, kz_ref, *refs):
    *parts, out_ref, half_ref = refs
    blur_into(kx_ref, ky_ref, kz_ref, parts, half_ref, out_ref)


def first_back_kernel(kx_ref, ky_ref, kz_ref, blurred_ref, *refs):
    tiles = refs[:SPAN]
    *outs, measured_ref, half_ref, edge_ref, peak_ref = refs[SPAN:]
    for k in range(SPAN):
        for c in range(CAP):
            code = tiles[k][CAP * TROWS :, :].astype(F32)[8 * c, 0].astype(jnp.int32)
            measured_ref[code] = tiles[k][c * TROWS : (c + 1) * TROWS, :]
    back_from(kx_ref, ky_ref, kz_ref, measured_ref, blurred_ref, half_ref, edge_ref, peak_ref, outs)


def sweep_kernel(*refs):
    fwd, back, parts = refs[0:3], refs[3:6], refs[6:10]
    measured_ref = refs[10]
    outs = refs[11:15]
    half_ref, edge_ref, peak_ref, blurred_ref = refs[15:]
    blur_into(*fwd, parts, half_ref, blurred_ref)
    back_from(*back, measured_ref, blurred_ref, half_ref, edge_ref, peak_ref, outs)


def join_kernel(own_ref, edge_ref, out_ref, sum_ref):
    scales = payload_scales(edge_ref)
    peaks = []
    for p in range(HX):
        plane = own_ref[p] + payload_plane(edge_ref, scales, p)
        sum_ref[p] = plane
        peaks.append(jnp.max(plane, axis=0, keepdims=True))
    write_payload(out_ref, sum_ref, jnp.concatenate(peaks, axis=0))


def update_planes(view_count, before_ref, own_ref, other_ref, out_refs):
    own, other = payload_scales(own_ref), payload_scales(other_ref)
    for p in range(HX):
        total = payload_plane(own_ref, own, p) + payload_plane(other_ref, other, p)
        plane = before_ref[p] * total * (1.0 / view_count)
        for ref in out_refs:
            ref[p] = plane.astype(ref.dtype)


def update_kernel(view_count, before_ref, own_ref, other_ref, *out_refs):
    update_planes(view_count, before_ref, own_ref, other_ref, out_refs)


def last_kernel(view_count, low_ref, high_ref, *refs):
    *payloads, out_ref = refs
    for i, before_ref in enumerate((low_ref, high_ref)):
        own_ref, other_ref = payloads[2 * i : 2 * i + 2]
        update_planes(view_count, before_ref, own_ref, other_ref, (out_ref.at[pl.ds(i * HX, HX)],))


VM = pl.BlockSpec(memory_space=pltpu.VMEM)
BLURRED = (VIEWS_DEV * BX // TP, TROWS, Z)
HALF_SHAPE = (VIEWS_DEV * BX, Y, Z)
PAYLOAD = jax.ShapeDtypeStruct((HX * Y + HX, Z), I16)
OWN = jax.ShapeDtypeStruct((HX, Y, Z), F32)
CONTRIB = [PAYLOAD, OWN, OWN, PAYLOAD]
BLUR_SCRATCH = [pltpu.VMEM(HALF_SHAPE, F32)]
BACK_SCRATCH = [
    pltpu.VMEM(HALF_SHAPE, F32),
    pltpu.VMEM((2, HX, Y, Z), F32),
    pltpu.VMEM((2, HX, 8, Z), F32),
]


def call(kernel, name, operands, out_shape, scratch, flops, vmem=6):
    return pl.pallas_call(
        kernel,
        out_shape=out_shape,
        in_specs=[VM] * len(operands),
        out_specs=jax.tree.map(lambda _: VM, out_shape),
        scratch_shapes=scratch,
        compiler_params=pltpu.CompilerParams(vmem_limit_bytes=vmem * MIB),
        cost_estimate=pl.CostEstimate(flops=flops, bytes_accessed=12 << 20, transcendentals=0),
        name=name,
    )(*operands)


def neighbours(low, high):
    size = lax.axis_size("block")
    up = [(i, i + 1) for i in range(size - 1)]
    down = [(j, i) for i, j in up]
    return lax.ppermute(high, "block", up), lax.ppermute(low, "block", down)


def exchanged(contributions):
    left, low, high, right = contributions
    pairs = []
    for own, edge in zip((low, high), neighbours(left, right)):
        payload = call(join_kernel, "join", (own, edge), PAYLOAD, [pltpu.VMEM(OWN.shape, F32)], 1 << 20)
        pairs.append((payload, lax.ppermute(payload, "view", [(0, 1), (1, 0)])))
    return pairs


def shards(estimate, view_tiles, tile_dest, psf_taps):
    view_count = psf_taps.shape[0] * lax.axis_size("view")
    blocks = lax.axis_size("block")
    packed = pack_tiles(view_tiles, tile_dest)
    estimate, psf_taps, packed = lax.optimization_barrier((estimate, psf_taps, packed))
    arrived = list(packed)

    def route(steps):
        for by in steps:
            perm = [(i, (i + by) % blocks) for i in range(blocks)]
            arrived[by + SPAN // 2] = lax.ppermute(packed[by + SPAN // 2], "block", perm)

    planes = estimate.astype(BF16)
    low, high = planes[:HX], planes[HX:]
    left, right = neighbours(low, high)
    route(EARLY)
    fwd, back = blur_matrices(psf_taps)
    blurred = call(
        first_blur_kernel,
        "first_blur",
        (*fwd, left, low, high, right),
        jax.ShapeDtypeStruct(BLURRED, F32),
        BLUR_SCRATCH,
        6 << 30,
        18,
    )
    packed, blurred = lax.optimization_barrier((packed, blurred))
    route(LATE)
    *contributions, measured = call(
        first_back_kernel,
        "first_back",
        (*back, blurred, *arrived),
        [*CONTRIB, jax.ShapeDtypeStruct((VIEWS_DEV * BX // TP, TROWS, Z), BF16)],
        BACK_SCRATCH,
        8 << 30,
        28,
    )
    halves = []
    for i, (own, other) in enumerate(exchanged(contributions)):
        halves.append(
            call(
                functools.partial(update_kernel, view_count),
                "update",
                (estimate[i * HX : (i + 1) * HX], own, other),
                [OWN, jax.ShapeDtypeStruct(OWN.shape, BF16)],
                [],
                1 << 20,
            )
        )
    (low, low_planes), (high, high_planes) = halves
    left, right = neighbours(low_planes, high_planes)
    contributions = call(
        sweep_kernel,
        "sweep",
        (*fwd, *back, left, low_planes, high_planes, right, measured),
        CONTRIB,
        [*BACK_SCRATCH, pltpu.VMEM(BLURRED, F32)],
        14 << 30,
        28,
    )
    payloads = [payload for pair in exchanged(contributions) for payload in pair]
    return call(
        functools.partial(last_kernel, view_count),
        "last_update",
        (low, high, *payloads),
        jax.ShapeDtypeStruct(estimate.shape, F32),
        [],
        1 << 20,
        10,
    )


def solution(mesh):
    return jax.shard_map(
        shards,
        mesh=mesh,
        in_specs=(
            P("block", None, None),
            P("view", "block", None, None, None),
            P("view", "block", None),
            P("view", None, None),
        ),
        out_specs=P("block", None, None),
        check_vma=False,
    )
```

```python
import functools

import jax
import jax.numpy as jnp
from jax import lax
from jax.experimental import pallas as pl
from jax.experimental.pallas import tpu as pltpu
from jax.sharding import PartitionSpec as P

TAPS = 31
HALF = TAPS // 2
BX = 32
HX = 16
CHUNKS = 4
CX = BX // CHUNKS
EDGES = HX // CX
EX = BX + 2 * HX
Y = 128
Z = 128
LANES = 128
VIEWS_DEV = 3
ITERS = 2
CAP = 2
SPAN = 12
TP = 4
SLOTS = SPAN * CAP
TROWS = TP * Y
PROWS = CAP * TROWS + 16
SUB = 16
F32 = jnp.float32
BF16 = jnp.bfloat16
I16 = jnp.int16
MIB = 1 << 20
UNROLL = 4
EARLY = (-6, 5, -5, 4, -4, 3, -3)
LATE = (2, -2, 1, -1)


def toeplitz(row, rows, shift, low, high):
    turned = pltpu.roll(
        jnp.broadcast_to(row, (rows, LANES)), shift % LANES, 1, stride=1, stride_axis=0
    )
    lag = lax.broadcasted_iota(jnp.int32, (rows, LANES), 1) - lax.broadcasted_iota(
        jnp.int32, (rows, LANES), 0
    )
    return jnp.where((lag >= low) & (lag <= high), turned, 0.0)


def prepare_kernel(psf_ref, *refs):
    *outs, taps_ref, turned_ref = refs
    fwd_x_ref, fwd_y_ref, fwd_z_ref, back_x_ref, back_y_ref, back_z_ref = outs
    dims = psf_ref.shape[1]
    taps_ref[...] = jnp.zeros(taps_ref.shape, F32)
    for v in range(VIEWS_DEV):
        taps = psf_ref[v]
        taps_ref[v * dims : (v + 1) * dims, :TAPS] = taps / jnp.sum(taps, axis=1, keepdims=True)
    turned_ref[...] = jnp.transpose(taps_ref[...])
    left_over = jnp.zeros((1, LANES), F32)
    for a in range(TAPS):
        wanted = turned_ref[a : a + 1, :] + left_over
        near = wanted.astype(BF16).astype(F32)
        left_over = wanted - near
        turned_ref[a : a + 1, :] = near
    taps_ref[...] = jnp.transpose(turned_ref[...])
    for a in range(TAPS):
        turned_ref[TAPS + 1 + a : TAPS + 2 + a, :] = turned_ref[TAPS - 1 - a : TAPS - a, :]
    turned_ref[:TAPS, :] = turned_ref[TAPS + 1 : 2 * TAPS + 1, :]
    turned_ref[TAPS:, :] = jnp.zeros((LANES - TAPS, LANES), F32)
    turned_ref[...] = jnp.transpose(turned_ref[...])
    wide = []
    for v in range(VIEWS_DEV):
        ahead = [taps_ref[v * dims + d : v * dims + d + 1, :] for d in range(dims)]
        behind = [turned_ref[v * dims + d : v * dims + d + 1, :] for d in range(dims)]
        wide.append(toeplitz(ahead[0], BX, 1, 1, TAPS))
        for ref, row in (
            (fwd_y_ref, ahead[1]),
            (back_y_ref, behind[1]),
            (fwd_z_ref, behind[2]),
            (back_z_ref, ahead[2]),
        ):
            ref[v] = toeplitz(row, LANES, -HALF, -HALF, HALF).astype(BF16)
    along = jnp.concatenate(wide, axis=0)
    fwd_x_ref[...] = along[:, :EX].astype(BF16)
    full = jnp.concatenate([along, jnp.zeros((LANES - VIEWS_DEV * BX, LANES), F32)], axis=0)
    across = jnp.transpose(full)[:EX, : VIEWS_DEV * BX].astype(BF16)
    back_x_ref[...] = jnp.concatenate([across, across], axis=1)


def blur_matrices(psf_taps):
    square = jax.ShapeDtypeStruct((VIEWS_DEV, LANES, LANES), BF16)
    shapes = [
        jax.ShapeDtypeStruct((VIEWS_DEV * BX, EX), BF16),
        square,
        square,
        jax.ShapeDtypeStruct((EX, 2 * VIEWS_DEV * BX), BF16),
        square,
        square,
    ]
    scratch = [pltpu.VMEM((LANES, LANES), F32)] * 2
    matrices = call(prepare_kernel, "prepare", (psf_taps,), shapes, scratch, 1 << 20)
    return matrices[:3], matrices[3:]


def pack_kernel(me_ref, dest_ref, tiles_ref, *refs):
    outs, (order_ref, count_ref) = refs[:SPAN], refs[SPAN:]
    me = me_ref[0]
    for k in range(SPAN):
        count_ref[k] = 0
    for n in range(SLOTS):
        step = lax.rem(dest_ref[n, 0] - me + SPAN // 2 + 64, 64)
        rank = count_ref[step]
        count_ref[step] = rank + 1
        order_ref[step * CAP + rank] = n
    for k in range(SPAN):
        codes = []
        for c in range(CAP):
            n = order_ref[k * CAP + c]
            outs[k][c * TROWS : (c + 1) * TROWS, :] = tiles_ref[n]
            code = dest_ref[n, 1] * (BX // TP) + dest_ref[n, 2]
            codes.append(jnp.full((8, Z), code, jnp.int32).astype(F32))
        outs[k][CAP * TROWS :, :] = jnp.concatenate(codes, axis=0).astype(BF16)


def pack_tiles(view_tiles, tile_dest):
    me = lax.axis_index("block").astype(jnp.int32).reshape(1)
    return pl.pallas_call(
        pack_kernel,
        out_shape=[jax.ShapeDtypeStruct((PROWS, Z), BF16)] * SPAN,
        in_specs=[
            pl.BlockSpec(memory_space=pltpu.SMEM),
            pl.BlockSpec(memory_space=pltpu.SMEM),
            pl.BlockSpec(memory_space=pltpu.VMEM),
        ],
        out_specs=[pl.BlockSpec(memory_space=pltpu.VMEM)] * SPAN,
        scratch_shapes=[pltpu.SMEM((SLOTS,), jnp.int32), pltpu.SMEM((SPAN,), jnp.int32)],
        compiler_params=pltpu.CompilerParams(vmem_limit_bytes=8 * MIB),
        cost_estimate=pl.CostEstimate(flops=0, bytes_accessed=2 * SLOTS * TROWS * Z * 2, transcendentals=0),
        name="pack_tiles",
    )(me, tile_dest[0], view_tiles.reshape(SLOTS, TROWS, Z))


STEPS = (64, 32, 16, 8, 4, 2, 1)
OFFSET = 64


def column_codes(peak):
    bound = peak * (2.0**-15 * (1 + 2.0**-12))
    scale = jnp.full(peak.shape, 2.0 ** (1 - OFFSET), F32)
    shrink = jnp.full(peak.shape, 2.0 ** (OFFSET - 1), F32)
    power = jnp.full(peak.shape, 1.0 - OFFSET, F32)
    for step in STEPS:
        larger = scale * 2.0 ** (step - 1) <= bound
        scale = jnp.where(larger, scale * 2.0**step, scale)
        shrink = jnp.where(larger, shrink * 2.0**-step, shrink)
        power = jnp.where(larger, power + step, power)
    return shrink, power


def column_scales(power):
    left = power + OFFSET
    scale = jnp.full(power.shape, 2.0**-OFFSET, F32)
    for step in STEPS:
        larger = left >= step
        scale = jnp.where(larger, scale * 2.0**step, scale)
        left = jnp.where(larger, left - step, left)
    return scale


def to_codes(values):
    return jnp.round(values).astype(jnp.int32).astype(I16)


def from_codes(codes):
    return codes.astype(jnp.int32).astype(F32)


def write_payload(ref, planes, peak):
    shrink, power = column_codes(peak)
    for p in range(CX):
        ref[p * Y : (p + 1) * Y, :] = to_codes(planes[p] * shrink[p : p + 1])
    ref[CX * Y :, :] = jnp.concatenate([power] * (16 // CX), axis=0).astype(jnp.int32).astype(I16)


def payload_scales(ref):
    return column_scales(from_codes(ref[CX * Y :, :]))


def payload_plane(ref, scales, p):
    return from_codes(ref[p * Y : (p + 1) * Y, :]) * scales[p : p + 1]


def swapped(block):
    return jnp.transpose(block, (1, 0, 2))


def blur_into(kx_ref, ky_ref, kz_ref, parts, half_ref, out_ref):
    def along_x(t, carry):
        y0 = pl.multiple_of(t * SUB, SUB)
        data = jnp.concatenate([ref[:, pl.ds(y0, SUB), :] for ref in parts], axis=0).astype(F32)
        for h in range(0, SUB, 8):
            rows = swapped(data[:, h : h + 8]).astype(BF16)
            outs = []
            for j in range(0, 8, 2):
                pair = jnp.concatenate([rows[j], rows[j + 1]], axis=1)
                got = jnp.dot(kx_ref[...], pair, preferred_element_type=F32)
                outs += [got[:, :Z], got[:, Z:]]
            half_ref[:, pl.ds(y0 + h, 8), :] = swapped(jnp.stack(outs, axis=0))
        return carry

    lax.fori_loop(0, Y // SUB, along_x, 0, unroll=2)

    def along_yz(q, carry):
        v = q // (BX // TP)
        outs = []
        for i in range(0, TP, 2):
            pair = jnp.concatenate(
                [half_ref[q * TP + i + j].astype(BF16) for j in range(2)], axis=1
            )
            got = jnp.dot(ky_ref[v], pair, preferred_element_type=F32).astype(BF16)
            outs += [got[:, :Z], got[:, Z:]]
        rows = jnp.concatenate(outs, axis=0)
        out_ref[q] = jnp.dot(rows, kz_ref[v], preferred_element_type=F32)
        return carry

    lax.fori_loop(0, VIEWS_DEV * BX // TP, along_yz, 0, unroll=UNROLL)


def back_from(kx_ref, ky_ref, kz_ref, measured_ref, blurred_ref, half_ref, edge_ref, peak_ref, outs):
    owns = outs[EDGES : EDGES + CHUNKS]

    def along_zy(q, carry):
        v = q // (BX // TP)
        ratio = (measured_ref[q].astype(F32) / blurred_ref[q]).astype(BF16)
        rows = jnp.dot(ratio, kz_ref[v], preferred_element_type=F32).astype(BF16)
        for i in range(0, TP, 2):
            pair = jnp.concatenate([rows[(i + j) * Y : (i + j + 1) * Y] for j in range(2)], axis=1)
            got = jnp.dot(ky_ref[v], pair, preferred_element_type=F32)
            for j in range(2):
                half_ref[q * TP + i + j] = got[:, j * Z : (j + 1) * Z]
        return carry

    lax.fori_loop(0, VIEWS_DEV * BX // TP, along_zy, 0, unroll=UNROLL)

    def along_x(t, carry):
        y0 = pl.multiple_of(t * 8, 8)
        data = swapped(half_ref[:, pl.ds(y0, 8), :])
        high = data.astype(BF16)
        low = (data - high.astype(F32)).astype(BF16)
        got = []
        for j in range(0, 8, 2):
            pair = [jnp.concatenate([part[j], part[j + 1]], axis=1) for part in (high, low)]
            both = jnp.dot(
                kx_ref[...], jnp.concatenate(pair, axis=0), preferred_element_type=F32
            )
            got += [both[:, :Z], both[:, Z:]]
        planes = swapped(jnp.stack(got, axis=0))
        for i, ref in enumerate(owns):
            ref[:, pl.ds(y0, 8), :] = planes[HX + i * CX : HX + (i + 1) * CX]
        edge_ref[0, :, pl.ds(y0, 8), :] = planes[:HX]
        edge_ref[1, :, pl.ds(y0, 8), :] = planes[HX + BX :]
        for i, part in enumerate((planes[:HX], planes[HX + BX :])):
            peak_ref[i] = jnp.maximum(peak_ref[i], part)
        return carry

    peak_ref[...] = jnp.zeros(peak_ref.shape, F32)
    lax.fori_loop(0, Y // 8, along_x, 0, unroll=UNROLL)
    for i, refs in enumerate((outs[:EDGES], outs[EDGES + CHUNKS :])):
        for c, ref in enumerate(refs):
            part = pl.ds(c * CX, CX)
            write_payload(ref, edge_ref.at[i, part], jnp.max(peak_ref[i, part], axis=1))


def first_blur_kernel(kx_ref, ky_ref, kz_ref, *refs):
    *parts, out_ref, half_ref = refs
    blur_into(kx_ref, ky_ref, kz_ref, parts, half_ref, out_ref)


def first_back_kernel(kx_ref, ky_ref, kz_ref, blurred_ref, *refs):
    tiles = refs[:SPAN]
    *outs, measured_ref, half_ref, edge_ref, peak_ref = refs[SPAN:]
    for k in range(SPAN):
        for c in range(CAP):
            code = tiles[k][CAP * TROWS :, :].astype(F32)[8 * c, 0].astype(jnp.int32)
            measured_ref[code] = tiles[k][c * TROWS : (c + 1) * TROWS, :]
    back_from(kx_ref, ky_ref, kz_ref, measured_ref, blurred_ref, half_ref, edge_ref, peak_ref, outs)


def sweep_kernel(*refs):
    fwd, back, parts = refs[0:3], refs[3:6], refs[6 : 6 + EX // CX]
    measured_ref, *outs, half_ref, edge_ref, peak_ref, blurred_ref = refs[6 + EX // CX :]
    blur_into(*fwd, parts, half_ref, blurred_ref)
    back_from(*back, measured_ref, blurred_ref, half_ref, edge_ref, peak_ref, outs)


def join_kernel(own_ref, edge_ref, out_ref, sum_ref):
    scales = payload_scales(edge_ref)
    peaks = []
    for p in range(CX):
        plane = own_ref[p] + payload_plane(edge_ref, scales, p)
        sum_ref[p] = plane
        peaks.append(jnp.max(plane, axis=0, keepdims=True))
    write_payload(out_ref, sum_ref, jnp.concatenate(peaks, axis=0))


def update_planes(view_count, before_ref, own_ref, other_ref, out_refs):
    own, other = payload_scales(own_ref), payload_scales(other_ref)
    for p in range(CX):
        total = payload_plane(own_ref, own, p) + payload_plane(other_ref, other, p)
        plane = before_ref[p] * total * (1.0 / view_count)
        for ref in out_refs:
            ref[p] = plane.astype(ref.dtype)


def update_kernel(view_count, before_ref, own_ref, other_ref, *out_refs):
    update_planes(view_count, before_ref, own_ref, other_ref, out_refs)


def last_kernel(view_count, *refs):
    *refs, out_ref = refs
    for i in range(CHUNKS):
        own_ref, other_ref = refs[CHUNKS + 2 * i : CHUNKS + 2 * i + 2]
        update_planes(view_count, refs[i], own_ref, other_ref, (out_ref.at[pl.ds(i * CX, CX)],))


VM = pl.BlockSpec(memory_space=pltpu.VMEM)
BLURRED = (VIEWS_DEV * BX // TP, TROWS, Z)
HALF_SHAPE = (VIEWS_DEV * BX, Y, Z)
PAYLOAD = jax.ShapeDtypeStruct((CX * Y + 16, Z), I16)
OWN = jax.ShapeDtypeStruct((CX, Y, Z), F32)
CONTRIB = [*[PAYLOAD] * EDGES, *[OWN] * CHUNKS, *[PAYLOAD] * EDGES]
BLUR_SCRATCH = [pltpu.VMEM(HALF_SHAPE, F32)]
BACK_SCRATCH = [
    pltpu.VMEM(HALF_SHAPE, F32),
    pltpu.VMEM((2, HX, Y, Z), F32),
    pltpu.VMEM((2, HX, 8, Z), F32),
]


def call(kernel, name, operands, out_shape, scratch, flops, vmem=6):
    return pl.pallas_call(
        kernel,
        out_shape=out_shape,
        in_specs=[VM] * len(operands),
        out_specs=jax.tree.map(lambda _: VM, out_shape),
        scratch_shapes=scratch,
        compiler_params=pltpu.CompilerParams(vmem_limit_bytes=vmem * MIB),
        cost_estimate=pl.CostEstimate(flops=flops, bytes_accessed=12 << 20, transcendentals=0),
        name=name,
    )(*operands)


def to_right(shard):
    size = lax.axis_size("block")
    return lax.ppermute(shard, "block", [(i, i + 1) for i in range(size - 1)])


def to_left(shard):
    size = lax.axis_size("block")
    return lax.ppermute(shard, "block", [(i + 1, i) for i in range(size - 1)])


def exchanged(contributions):
    owns = contributions[EDGES : EDGES + CHUNKS]
    arrived = [None] * CHUNKS
    for c in range(EDGES):
        arrived[c] = to_right(contributions[EDGES + CHUNKS + c])
        arrived[CHUNKS - EDGES + c] = to_left(contributions[c])
    pairs = []
    for own, edge in zip(owns, arrived):
        payload = call(join_kernel, "join", (own, edge), PAYLOAD, [pltpu.VMEM(OWN.shape, F32)], 1 << 20)
        pairs.append((payload, lax.ppermute(payload, "view", [(0, 1), (1, 0)])))
    return pairs


def shards(estimate, view_tiles, tile_dest, psf_taps):
    view_count = psf_taps.shape[0] * lax.axis_size("view")
    blocks = lax.axis_size("block")
    packed = pack_tiles(view_tiles, tile_dest)
    estimate, psf_taps, packed = lax.optimization_barrier((estimate, psf_taps, packed))
    arrived = list(packed)

    def route(steps):
        for by in steps:
            perm = [(i, (i + by) % blocks) for i in range(blocks)]
            arrived[by + SPAN // 2] = lax.ppermute(packed[by + SPAN // 2], "block", perm)

    planes = estimate.astype(BF16)
    low, high = planes[:HX], planes[HX:]
    left, right = to_right(high), to_left(low)
    route(EARLY)
    fwd, back = blur_matrices(psf_taps)
    blurred = call(
        first_blur_kernel,
        "first_blur",
        (*fwd, left, low, high, right),
        jax.ShapeDtypeStruct(BLURRED, F32),
        BLUR_SCRATCH,
        6 << 30,
        18,
    )
    packed, blurred = lax.optimization_barrier((packed, blurred))
    route(LATE)
    *contributions, measured = call(
        first_back_kernel,
        "first_back",
        (*back, blurred, *arrived),
        [*CONTRIB, jax.ShapeDtypeStruct((VIEWS_DEV * BX // TP, TROWS, Z), BF16)],
        BACK_SCRATCH,
        8 << 30,
        28,
    )
    chunks = []
    for i, (own, other) in enumerate(exchanged(contributions)):
        chunks.append(
            call(
                functools.partial(update_kernel, view_count),
                "update",
                (estimate[i * CX : (i + 1) * CX], own, other),
                [OWN, jax.ShapeDtypeStruct(OWN.shape, BF16)],
                [],
                1 << 20,
            )
        )
    planes = [chunk[1] for chunk in chunks]
    left = [to_right(part) for part in planes[CHUNKS - EDGES :]]
    right = [to_left(part) for part in planes[:EDGES]]
    contributions = call(
        sweep_kernel,
        "sweep",
        (*fwd, *back, *left, *planes, *right, measured),
        CONTRIB,
        [*BACK_SCRATCH, pltpu.VMEM(BLURRED, F32)],
        14 << 30,
        28,
    )
    payloads = [payload for pair in exchanged(contributions) for payload in pair]
    return call(
        functools.partial(last_kernel, view_count),
        "last_update",
        (*[chunk[0] for chunk in chunks], *payloads),
        jax.ShapeDtypeStruct(estimate.shape, F32),
        [],
        1 << 20,
        10,
    )


def solution(mesh):
    return jax.shard_map(
        shards,
        mesh=mesh,
        in_specs=(
            P("block", None, None),
            P("view", "block", None, None, None),
            P("view", "block", None),
            P("view", None, None),
        ),
        out_specs=P("block", None, None),
        check_vma=False,
    )
```

```python
import functools

import jax
import jax.numpy as jnp
from jax import lax
from jax.experimental import pallas as pl
from jax.experimental.pallas import tpu as pltpu
from jax.sharding import PartitionSpec as P

TAPS = 31
HALF = TAPS // 2
BX = 32
HX = 16
EX = BX + 2 * HX
Y = 128
Z = 128
LANES = 128
VIEWS_DEV = 3
ITERS = 2
CAP = 2
SPAN = 12
TP = 4
SLOTS = SPAN * CAP
TROWS = TP * Y
PROWS = CAP * TROWS + 16
SUB = 16
F32 = jnp.float32
BF16 = jnp.bfloat16
I16 = jnp.int16
MIB = 1 << 20
UNROLL = 12
EARLY = (-6, 5, -5, 4, -4, 3, -3)
LATE = (2, -2, 1, -1)


def toeplitz(row, rows, shift, low, high):
    turned = pltpu.roll(
        jnp.broadcast_to(row, (rows, LANES)), shift % LANES, 1, stride=1, stride_axis=0
    )
    lag = lax.broadcasted_iota(jnp.int32, (rows, LANES), 1) - lax.broadcasted_iota(
        jnp.int32, (rows, LANES), 0
    )
    return jnp.where((lag >= low) & (lag <= high), turned, 0.0)


def prepare_kernel(psf_ref, *refs):
    *outs, taps_ref, turned_ref = refs
    fwd_x_ref, fwd_y_ref, fwd_z_ref, back_x_ref, back_y_ref, back_z_ref = outs
    dims = psf_ref.shape[1]
    taps_ref[...] = jnp.zeros(taps_ref.shape, F32)
    for v in range(VIEWS_DEV):
        taps = psf_ref[v]
        taps_ref[v * dims : (v + 1) * dims, :TAPS] = taps / jnp.sum(taps, axis=1, keepdims=True)
    turned_ref[...] = jnp.transpose(taps_ref[...])
    left_over = jnp.zeros((1, LANES), F32)
    for a in range(TAPS):
        wanted = turned_ref[a : a + 1, :] + left_over
        near = wanted.astype(BF16).astype(F32)
        left_over = wanted - near
        turned_ref[a : a + 1, :] = near
    taps_ref[...] = jnp.transpose(turned_ref[...])
    for a in range(TAPS):
        turned_ref[TAPS + 1 + a : TAPS + 2 + a, :] = turned_ref[TAPS - 1 - a : TAPS - a, :]
    turned_ref[:TAPS, :] = turned_ref[TAPS + 1 : 2 * TAPS + 1, :]
    turned_ref[TAPS:, :] = jnp.zeros((LANES - TAPS, LANES), F32)
    turned_ref[...] = jnp.transpose(turned_ref[...])
    wide = []
    for v in range(VIEWS_DEV):
        ahead = [taps_ref[v * dims + d : v * dims + d + 1, :] for d in range(dims)]
        behind = [turned_ref[v * dims + d : v * dims + d + 1, :] for d in range(dims)]
        wide.append(toeplitz(ahead[0], BX, 1, 1, TAPS))
        for ref, row in ((fwd_y_ref, ahead[1]), (back_y_ref, behind[1])):
            ref[v] = toeplitz(row, LANES, -HALF, -HALF, HALF).astype(BF16)
        for ref, row in ((fwd_z_ref, behind[2]), (back_z_ref, ahead[2])):
            block = toeplitz(row, LANES, -HALF, -HALF, HALF).astype(BF16)
            ref[v] = jnp.zeros(ref.shape[1:], BF16)
            ref[v, :LANES, :LANES] = block
            ref[v, LANES:, LANES:] = block
    along = jnp.concatenate(wide, axis=0)
    fwd_x_ref[...] = along[:, :EX].astype(BF16)
    full = jnp.concatenate([along, jnp.zeros((LANES - VIEWS_DEV * BX, LANES), F32)], axis=0)
    across = jnp.transpose(full)[:EX, : VIEWS_DEV * BX].astype(BF16)
    back_x_ref[...] = jnp.concatenate([across, across], axis=1)


def blur_matrices(psf_taps):
    square = jax.ShapeDtypeStruct((VIEWS_DEV, LANES, LANES), BF16)
    double = jax.ShapeDtypeStruct((VIEWS_DEV, 2 * LANES, 2 * LANES), BF16)
    shapes = [
        jax.ShapeDtypeStruct((VIEWS_DEV * BX, EX), BF16),
        square,
        double,
        jax.ShapeDtypeStruct((EX, 2 * VIEWS_DEV * BX), BF16),
        square,
        double,
    ]
    scratch = [pltpu.VMEM((LANES, LANES), F32)] * 2
    matrices = call(prepare_kernel, "prepare", (psf_taps,), shapes, scratch, 1 << 20)
    return matrices[:3], matrices[3:]


def pack_kernel(me_ref, dest_ref, tiles_ref, *refs):
    outs, (order_ref, count_ref) = refs[:SPAN], refs[SPAN:]
    me = me_ref[0]
    for k in range(SPAN):
        count_ref[k] = 0
    for n in range(SLOTS):
        step = lax.rem(dest_ref[n, 0] - me + SPAN // 2 + 64, 64)
        rank = count_ref[step]
        count_ref[step] = rank + 1
        order_ref[step * CAP + rank] = n
    for k in range(SPAN):
        codes = []
        for c in range(CAP):
            n = order_ref[k * CAP + c]
            outs[k][c * TROWS : (c + 1) * TROWS, :] = tiles_ref[n]
            code = dest_ref[n, 1] * (BX // TP) + dest_ref[n, 2]
            codes.append(jnp.full((8, Z), code, jnp.int32).astype(F32))
        outs[k][CAP * TROWS :, :] = jnp.concatenate(codes, axis=0).astype(BF16)


def pack_tiles(view_tiles, tile_dest):
    me = lax.axis_index("block").astype(jnp.int32).reshape(1)
    return pl.pallas_call(
        pack_kernel,
        out_shape=[jax.ShapeDtypeStruct((PROWS, Z), BF16)] * SPAN,
        in_specs=[
            pl.BlockSpec(memory_space=pltpu.SMEM),
            pl.BlockSpec(memory_space=pltpu.SMEM),
            pl.BlockSpec(memory_space=pltpu.VMEM),
        ],
        out_specs=[pl.BlockSpec(memory_space=pltpu.VMEM)] * SPAN,
        scratch_shapes=[pltpu.SMEM((SLOTS,), jnp.int32), pltpu.SMEM((SPAN,), jnp.int32)],
        compiler_params=pltpu.CompilerParams(vmem_limit_bytes=8 * MIB),
        cost_estimate=pl.CostEstimate(flops=0, bytes_accessed=2 * SLOTS * TROWS * Z * 2, transcendentals=0),
        name="pack_tiles",
    )(me, tile_dest[0], view_tiles.reshape(SLOTS, TROWS, Z))


STEPS = (64, 32, 16, 8, 4, 2, 1)
OFFSET = 64


def column_codes(peak):
    bound = peak * (2.0**-15 * (1 + 2.0**-12))
    scale = jnp.full(peak.shape, 2.0 ** (1 - OFFSET), F32)
    shrink = jnp.full(peak.shape, 2.0 ** (OFFSET - 1), F32)
    power = jnp.full(peak.shape, 1.0 - OFFSET, F32)
    for step in STEPS:
        larger = scale * 2.0 ** (step - 1) <= bound
        scale = jnp.where(larger, scale * 2.0**step, scale)
        shrink = jnp.where(larger, shrink * 2.0**-step, shrink)
        power = jnp.where(larger, power + step, power)
    return shrink, power


def column_scales(power):
    left = power + OFFSET
    scale = jnp.full(power.shape, 2.0**-OFFSET, F32)
    for step in STEPS:
        larger = left >= step
        scale = jnp.where(larger, scale * 2.0**step, scale)
        left = jnp.where(larger, left - step, left)
    return scale


def to_codes(values):
    return jnp.round(values).astype(jnp.int32).astype(I16)


def from_codes(codes):
    return codes.astype(jnp.int32).astype(F32)


def write_payload(ref, planes, peak):
    shrink, power = column_codes(peak)
    for p in range(HX):
        ref[p * Y : (p + 1) * Y, :] = to_codes(planes[p] * shrink[p : p + 1])
    ref[HX * Y :, :] = power.astype(jnp.int32).astype(I16)


def payload_scales(ref):
    return column_scales(from_codes(ref[HX * Y :, :]))


def payload_plane(ref, scales, p):
    return from_codes(ref[p * Y : (p + 1) * Y, :]) * scales[p : p + 1]


def swapped(block):
    return jnp.transpose(block, (1, 0, 2))


def blur_into(kx_ref, ky_ref, kz_ref, parts, half_ref, out_ref):
    def along_x(t, carry):
        y0 = pl.multiple_of(t * SUB, SUB)
        data = jnp.concatenate([ref[:, pl.ds(y0, SUB), :] for ref in parts], axis=0).astype(F32)
        planes = []
        for h in range(0, SUB, 8):
            rows = swapped(data[:, h : h + 8]).astype(BF16)
            outs = []
            for j in range(0, 8, 2):
                pair = jnp.concatenate([rows[j], rows[j + 1]], axis=1)
                got = jnp.dot(kx_ref[...], pair, preferred_element_type=F32)
                outs += [got[:, :Z], got[:, Z:]]
            planes.append(swapped(jnp.stack(outs, axis=0)))
        half_ref[:, pl.ds(y0, SUB), :] = jnp.concatenate(planes, axis=1).astype(half_ref.dtype)
        return carry

    lax.fori_loop(0, Y // SUB, along_x, 0, unroll=2)

    def along_yz(q, carry):
        v = q // (BX // TP)
        outs = []
        for i in range(0, TP, 2):
            pair = jnp.concatenate([half_ref[q * TP + i + j].astype(BF16) for j in range(2)], axis=1)
            outs.append(jnp.dot(ky_ref[v], pair, preferred_element_type=F32).astype(BF16))
        got = jnp.dot(jnp.concatenate(outs, axis=0), kz_ref[v], preferred_element_type=F32)
        for i in range(TP):
            rows, lanes = i // 2 * Y, i % 2 * Z
            out_ref[q, i * Y : (i + 1) * Y, :] = got[rows : rows + Y, lanes : lanes + Z]
        return carry

    lax.fori_loop(0, VIEWS_DEV * BX // TP, along_yz, 0, unroll=UNROLL)


def back_from(kx_ref, ky_ref, kz_ref, measured_ref, blurred_ref, half_ref, edge_ref, peak_ref, outs):
    left_ref, low_ref, high_ref, right_ref = outs

    def along_zy(q, carry):
        v = q // (BX // TP)
        ratio = (measured_ref[q].astype(F32) / blurred_ref[q]).astype(BF16)
        pairs = [
            jnp.concatenate([ratio[(i + j) * Y : (i + j + 1) * Y] for j in range(2)], axis=1)
            for i in range(0, TP, 2)
        ]
        rows = jnp.dot(
            jnp.concatenate(pairs, axis=0), kz_ref[v], preferred_element_type=F32
        ).astype(BF16)
        for i in range(0, TP, 2):
            pair = rows[i // 2 * Y : (i // 2 + 1) * Y]
            got = jnp.dot(ky_ref[v], pair, preferred_element_type=F32)
            for j in range(2):
                half_ref[q * TP + i + j] = got[:, j * Z : (j + 1) * Z]
        return carry

    lax.fori_loop(0, VIEWS_DEV * BX // TP, along_zy, 0, unroll=UNROLL)

    def along_x(t, carry):
        y0 = pl.multiple_of(t * 8, 8)
        data = swapped(half_ref[:, pl.ds(y0, 8), :])
        high = data.astype(BF16)
        low = (data - high.astype(F32)).astype(BF16)
        got = []
        for j in range(0, 8, 2):
            pair = [jnp.concatenate([part[j], part[j + 1]], axis=1) for part in (high, low)]
            both = jnp.dot(
                kx_ref[...], jnp.concatenate(pair, axis=0), preferred_element_type=F32
            )
            got += [both[:, :Z], both[:, Z:]]
        planes = swapped(jnp.stack(got, axis=0))
        for i, ref in enumerate((edge_ref.at[0], low_ref, high_ref, edge_ref.at[1])):
            ref[:, pl.ds(y0, 8), :] = planes[i * HX : (i + 1) * HX]
        for i, part in enumerate((planes[:HX], planes[HX + BX :])):
            peak_ref[i] = jnp.maximum(peak_ref[i], part)
        return carry

    peak_ref[...] = jnp.zeros(peak_ref.shape, F32)
    lax.fori_loop(0, Y // 8, along_x, 0, unroll=8)
    for i, ref in enumerate((left_ref, right_ref)):
        write_payload(ref, edge_ref.at[i], jnp.max(peak_ref[i], axis=1))


def first_blur_kernel(kx_ref, ky_ref, kz_ref, *refs):
    *parts, out_ref, half_ref = refs
    blur_into(kx_ref, ky_ref, kz_ref, parts, half_ref, out_ref)


def first_back_kernel(kx_ref, ky_ref, kz_ref, blurred_ref, *refs):
    tiles = refs[:SPAN]
    *outs, measured_ref, half_ref, edge_ref, peak_ref = refs[SPAN:]
    for k in range(SPAN):
        for c in range(CAP):
            code = tiles[k][CAP * TROWS :, :].astype(F32)[8 * c, 0].astype(jnp.int32)
            measured_ref[code] = tiles[k][c * TROWS : (c + 1) * TROWS, :]
    back_from(kx_ref, ky_ref, kz_ref, measured_ref, blurred_ref, half_ref, edge_ref, peak_ref, outs)


def sweep_kernel(*refs):
    fwd, back, parts = refs[0:3], refs[3:6], refs[6:10]
    measured_ref = refs[10]
    outs = refs[11:15]
    half_ref, edge_ref, peak_ref, blurred_ref = refs[15:]
    blur_into(*fwd, parts, half_ref, blurred_ref)
    back_from(*back, measured_ref, blurred_ref, half_ref, edge_ref, peak_ref, outs)


def join_kernel(own_ref, edge_ref, out_ref, sum_ref):
    scales = payload_scales(edge_ref)
    peaks = []
    for p in range(HX):
        plane = own_ref[p] + payload_plane(edge_ref, scales, p)
        sum_ref[p] = plane
        peaks.append(jnp.max(plane, axis=0, keepdims=True))
    write_payload(out_ref, sum_ref, jnp.concatenate(peaks, axis=0))


def update_planes(view_count, before_ref, own_ref, other_ref, out_refs):
    own, other = payload_scales(own_ref), payload_scales(other_ref)
    for p in range(HX):
        total = payload_plane(own_ref, own, p) + payload_plane(other_ref, other, p)
        plane = before_ref[p] * total * (1.0 / view_count)
        for ref in out_refs:
            ref[p] = plane.astype(ref.dtype)


def update_kernel(view_count, before_ref, own_ref, other_ref, *out_refs):
    update_planes(view_count, before_ref, own_ref, other_ref, out_refs)


def last_kernel(view_count, low_ref, high_ref, *refs):
    *payloads, out_ref = refs
    for i, before_ref in enumerate((low_ref, high_ref)):
        own_ref, other_ref = payloads[2 * i : 2 * i + 2]
        update_planes(view_count, before_ref, own_ref, other_ref, (out_ref.at[pl.ds(i * HX, HX)],))


VM = pl.BlockSpec(memory_space=pltpu.VMEM)
BLURRED = (VIEWS_DEV * BX // TP, TROWS, Z)
HALF_SHAPE = (VIEWS_DEV * BX, Y, Z)
PAYLOAD = jax.ShapeDtypeStruct((HX * Y + HX, Z), I16)
OWN = jax.ShapeDtypeStruct((HX, Y, Z), F32)
CONTRIB = [PAYLOAD, OWN, OWN, PAYLOAD]
BLUR_SCRATCH = [pltpu.VMEM(HALF_SHAPE, BF16)]
BACK_SCRATCH = [
    pltpu.VMEM(HALF_SHAPE, F32),
    pltpu.VMEM((2, HX, Y, Z), F32),
    pltpu.VMEM((2, HX, 8, Z), F32),
]


def call(kernel, name, operands, out_shape, scratch, flops, vmem=6):
    return pl.pallas_call(
        kernel,
        out_shape=out_shape,
        in_specs=[VM] * len(operands),
        out_specs=jax.tree.map(lambda _: VM, out_shape),
        scratch_shapes=scratch,
        compiler_params=pltpu.CompilerParams(vmem_limit_bytes=vmem * MIB),
        cost_estimate=pl.CostEstimate(flops=flops, bytes_accessed=12 << 20, transcendentals=0),
        name=name,
    )(*operands)


def neighbours(low, high):
    size = lax.axis_size("block")
    up = [(i, i + 1) for i in range(size - 1)]
    down = [(j, i) for i, j in up]
    return lax.ppermute(high, "block", up), lax.ppermute(low, "block", down)


def exchanged(contributions):
    left, low, high, right = contributions
    pairs = []
    for own, edge in zip((low, high), neighbours(left, right)):
        payload = call(join_kernel, "join", (own, edge), PAYLOAD, [pltpu.VMEM(OWN.shape, F32)], 1 << 20)
        pairs.append((payload, lax.ppermute(payload, "view", [(0, 1), (1, 0)])))
    return pairs


def shards(estimate, view_tiles, tile_dest, psf_taps):
    view_count = psf_taps.shape[0] * lax.axis_size("view")
    blocks = lax.axis_size("block")
    packed = pack_tiles(view_tiles, tile_dest)
    arrived = list(packed)

    def route(steps):
        for by in steps:
            perm = [(i, (i + by) % blocks) for i in range(blocks)]
            arrived[by + SPAN // 2] = lax.ppermute(packed[by + SPAN // 2], "block", perm)

    planes = estimate.astype(BF16)
    low, high = planes[:HX], planes[HX:]
    left, right = neighbours(low, high)
    route(EARLY)
    fwd, back = blur_matrices(psf_taps)
    blurred = call(
        first_blur_kernel,
        "first_blur",
        (*fwd, left, low, high, right),
        jax.ShapeDtypeStruct(BLURRED, F32),
        BLUR_SCRATCH,
        6 << 30,
        18,
    )
    packed, blurred = lax.optimization_barrier((packed, blurred))
    route(LATE)
    *contributions, measured = call(
        first_back_kernel,
        "first_back",
        (*back, blurred, *arrived),
        [*CONTRIB, jax.ShapeDtypeStruct((VIEWS_DEV * BX // TP, TROWS, Z), BF16)],
        BACK_SCRATCH,
        8 << 30,
        28,
    )
    halves = []
    for i, (own, other) in enumerate(exchanged(contributions)):
        halves.append(
            call(
                functools.partial(update_kernel, view_count),
                "update",
                (estimate[i * HX : (i + 1) * HX], own, other),
                [OWN, jax.ShapeDtypeStruct(OWN.shape, BF16)],
                [],
                1 << 20,
            )
        )
    (low, low_planes), (high, high_planes) = halves
    left, right = neighbours(low_planes, high_planes)
    contributions = call(
        sweep_kernel,
        "sweep",
        (*fwd, *back, left, low_planes, high_planes, right, measured),
        CONTRIB,
        [*BACK_SCRATCH, pltpu.VMEM(BLURRED, F32)],
        14 << 30,
        28,
    )
    payloads = [payload for pair in exchanged(contributions) for payload in pair]
    return call(
        functools.partial(last_kernel, view_count),
        "last_update",
        (low, high, *payloads),
        jax.ShapeDtypeStruct(estimate.shape, F32),
        [],
        1 << 20,
        10,
    )


def solution(mesh):
    return jax.shard_map(
        shards,
        mesh=mesh,
        in_specs=(
            P("block", None, None),
            P("view", "block", None, None, None),
            P("view", "block", None),
            P("view", None, None),
        ),
        out_specs=P("block", None, None),
        check_vma=False,
    )
```

```python
import functools

import jax
import jax.numpy as jnp
from jax import lax
from jax.experimental import pallas as pl
from jax.experimental.pallas import tpu as pltpu
from jax.sharding import PartitionSpec as P

TAPS = 31
HALF = TAPS // 2
BX = 32
HX = 16
EX = BX + 2 * HX
Y = 128
Z = 128
LANES = 128
VIEWS_DEV = 3
ITERS = 2
CAP = 2
SPAN = 12
TP = 4
SLOTS = SPAN * CAP
TROWS = TP * Y
PROWS = CAP * TROWS + 16
SUB = 16
F32 = jnp.float32
BF16 = jnp.bfloat16
I16 = jnp.int16
MIB = 1 << 20
UNROLL = 12
EARLY = (-6, 5, -5, 4, -4, 3, -3)
LATE = (2, -2, 1, -1)


def toeplitz(row, rows, shift, low, high):
    turned = pltpu.roll(
        jnp.broadcast_to(row, (rows, LANES)), shift % LANES, 1, stride=1, stride_axis=0
    )
    lag = lax.broadcasted_iota(jnp.int32, (rows, LANES), 1) - lax.broadcasted_iota(
        jnp.int32, (rows, LANES), 0
    )
    return jnp.where((lag >= low) & (lag <= high), turned, 0.0)


def prepare_kernel(psf_ref, *refs):
    *outs, taps_ref, turned_ref = refs
    fwd_x_ref, fwd_y_ref, fwd_z_ref, back_x_ref, back_y_ref, back_z_ref = outs
    dims = psf_ref.shape[1]
    taps_ref[...] = jnp.zeros(taps_ref.shape, F32)
    for v in range(VIEWS_DEV):
        taps = psf_ref[v]
        taps_ref[v * dims : (v + 1) * dims, :TAPS] = taps / jnp.sum(taps, axis=1, keepdims=True)
    turned_ref[...] = jnp.transpose(taps_ref[...])
    left_over = jnp.zeros((1, LANES), F32)
    for a in range(TAPS):
        wanted = turned_ref[a : a + 1, :] + left_over
        near = wanted.astype(BF16).astype(F32)
        left_over = wanted - near
        turned_ref[a : a + 1, :] = near
    taps_ref[...] = jnp.transpose(turned_ref[...])
    for a in range(TAPS):
        turned_ref[TAPS + 1 + a : TAPS + 2 + a, :] = turned_ref[TAPS - 1 - a : TAPS - a, :]
    turned_ref[:TAPS, :] = turned_ref[TAPS + 1 : 2 * TAPS + 1, :]
    turned_ref[TAPS:, :] = jnp.zeros((LANES - TAPS, LANES), F32)
    turned_ref[...] = jnp.transpose(turned_ref[...])
    wide = []
    for v in range(VIEWS_DEV):
        ahead = [taps_ref[v * dims + d : v * dims + d + 1, :] for d in range(dims)]
        behind = [turned_ref[v * dims + d : v * dims + d + 1, :] for d in range(dims)]
        wide.append(toeplitz(ahead[0], BX, 1, 1, TAPS))
        for ref, row in ((fwd_y_ref, ahead[1]), (back_y_ref, behind[1])):
            ref[v] = toeplitz(row, LANES, -HALF, -HALF, HALF).astype(BF16)
        for ref, row in ((fwd_z_ref, behind[2]), (back_z_ref, ahead[2])):
            block = toeplitz(row, LANES, -HALF, -HALF, HALF).astype(BF16)
            ref[v] = jnp.zeros(ref.shape[1:], BF16)
            ref[v, :LANES, :LANES] = block
            ref[v, LANES:, LANES:] = block
    along = jnp.concatenate(wide, axis=0)
    fwd_x_ref[...] = along[:, :EX].astype(BF16)
    full = jnp.concatenate([along, jnp.zeros((LANES - VIEWS_DEV * BX, LANES), F32)], axis=0)
    across = jnp.transpose(full)[:EX, : VIEWS_DEV * BX].astype(BF16)
    back_x_ref[...] = jnp.concatenate([across, across], axis=1)


def blur_matrices(psf_taps):
    square = jax.ShapeDtypeStruct((VIEWS_DEV, LANES, LANES), BF16)
    double = jax.ShapeDtypeStruct((VIEWS_DEV, 2 * LANES, 2 * LANES), BF16)
    shapes = [
        jax.ShapeDtypeStruct((VIEWS_DEV * BX, EX), BF16),
        square,
        double,
        jax.ShapeDtypeStruct((EX, 2 * VIEWS_DEV * BX), BF16),
        square,
        double,
    ]
    scratch = [pltpu.VMEM((LANES, LANES), F32)] * 2
    matrices = call(prepare_kernel, "prepare", (psf_taps,), shapes, scratch, 1 << 20)
    return matrices[:3], matrices[3:]


def pack_kernel(me_ref, dest_ref, tiles_ref, *refs):
    outs, (order_ref, count_ref) = refs[:SPAN], refs[SPAN:]
    me = me_ref[0]
    for k in range(SPAN):
        count_ref[k] = 0
    for n in range(SLOTS):
        step = lax.rem(dest_ref[n, 0] - me + SPAN // 2 + 64, 64)
        rank = count_ref[step]
        count_ref[step] = rank + 1
        order_ref[step * CAP + rank] = n
    for k in range(SPAN):
        codes = []
        for c in range(CAP):
            n = order_ref[k * CAP + c]
            outs[k][c * TROWS : (c + 1) * TROWS, :] = tiles_ref[n]
            code = dest_ref[n, 1] * (BX // TP) + dest_ref[n, 2]
            codes.append(jnp.full((8, Z), code, jnp.int32).astype(F32))
        outs[k][CAP * TROWS :, :] = jnp.concatenate(codes, axis=0).astype(BF16)


def pack_tiles(view_tiles, tile_dest):
    me = lax.axis_index("block").astype(jnp.int32).reshape(1)
    return pl.pallas_call(
        pack_kernel,
        out_shape=[jax.ShapeDtypeStruct((PROWS, Z), BF16)] * SPAN,
        in_specs=[
            pl.BlockSpec(memory_space=pltpu.SMEM),
            pl.BlockSpec(memory_space=pltpu.SMEM),
            pl.BlockSpec(memory_space=pltpu.VMEM),
        ],
        out_specs=[pl.BlockSpec(memory_space=pltpu.VMEM)] * SPAN,
        scratch_shapes=[pltpu.SMEM((SLOTS,), jnp.int32), pltpu.SMEM((SPAN,), jnp.int32)],
        compiler_params=pltpu.CompilerParams(vmem_limit_bytes=8 * MIB),
        cost_estimate=pl.CostEstimate(flops=0, bytes_accessed=2 * SLOTS * TROWS * Z * 2, transcendentals=0),
        name="pack_tiles",
    )(me, tile_dest[0], view_tiles.reshape(SLOTS, TROWS, Z))


STEPS = (64, 32, 16, 8, 4, 2, 1)
OFFSET = 64


def column_codes(peak):
    bound = peak * (2.0**-15 * (1 + 2.0**-12))
    scale = jnp.full(peak.shape, 2.0 ** (1 - OFFSET), F32)
    shrink = jnp.full(peak.shape, 2.0 ** (OFFSET - 1), F32)
    power = jnp.full(peak.shape, 1.0 - OFFSET, F32)
    for step in STEPS:
        larger = scale * 2.0 ** (step - 1) <= bound
        scale = jnp.where(larger, scale * 2.0**step, scale)
        shrink = jnp.where(larger, shrink * 2.0**-step, shrink)
        power = jnp.where(larger, power + step, power)
    return shrink, power


def column_scales(power):
    left = power + OFFSET
    scale = jnp.full(power.shape, 2.0**-OFFSET, F32)
    for step in STEPS:
        larger = left >= step
        scale = jnp.where(larger, scale * 2.0**step, scale)
        left = jnp.where(larger, left - step, left)
    return scale


def to_codes(values):
    return jnp.round(values).astype(jnp.int32).astype(I16)


def from_codes(codes):
    return codes.astype(jnp.int32).astype(F32)


def write_payload(ref, planes, peak):
    shrink, power = column_codes(peak)
    for p in range(HX):
        ref[p * Y : (p + 1) * Y, :] = to_codes(planes[p] * shrink[p : p + 1])
    ref[HX * Y :, :] = power.astype(jnp.int32).astype(I16)


def payload_scales(ref):
    return column_scales(from_codes(ref[HX * Y :, :]))


def payload_plane(ref, scales, p):
    return from_codes(ref[p * Y : (p + 1) * Y, :]) * scales[p : p + 1]


def swapped(block):
    return jnp.transpose(block, (1, 0, 2))


def blur_into(kx_ref, ky_ref, kz_ref, parts, half_ref, out_ref):
    def along_x(t, carry):
        y0 = pl.multiple_of(t * SUB, SUB)
        data = jnp.concatenate([ref[:, pl.ds(y0, SUB), :] for ref in parts], axis=0).astype(F32)
        planes = []
        for h in range(0, SUB, 8):
            rows = swapped(data[:, h : h + 8]).astype(BF16)
            outs = []
            for j in range(0, 8, 2):
                pair = jnp.concatenate([rows[j], rows[j + 1]], axis=1)
                got = jnp.dot(kx_ref[...], pair, preferred_element_type=F32)
                outs += [got[:, :Z], got[:, Z:]]
            planes.append(swapped(jnp.stack(outs, axis=0)))
        half_ref[:, pl.ds(y0, SUB), :] = jnp.concatenate(planes, axis=1).astype(half_ref.dtype)
        return carry

    lax.fori_loop(0, Y // SUB, along_x, 0, unroll=2)

    def along_yz(q, carry):
        v = q // (BX // TP)
        outs = []
        for i in range(0, TP, 2):
            pair = jnp.concatenate([half_ref[q * TP + i + j].astype(BF16) for j in range(2)], axis=1)
            outs.append(jnp.dot(ky_ref[v], pair, preferred_element_type=F32).astype(BF16))
        got = jnp.dot(jnp.concatenate(outs, axis=0), kz_ref[v], preferred_element_type=F32)
        for i in range(TP):
            rows, lanes = i // 2 * Y, i % 2 * Z
            out_ref[q, i * Y : (i + 1) * Y, :] = got[rows : rows + Y, lanes : lanes + Z]
        return carry

    lax.fori_loop(0, VIEWS_DEV * BX // TP, along_yz, 0, unroll=UNROLL)


def times_rows(taps, rows):
    got = []
    for j in range(0, 8, 2):
        pair = jnp.concatenate([rows[j], rows[j + 1]], axis=1)
        both = jnp.dot(taps, pair, preferred_element_type=F32)
        got += [both[:, :Z], both[:, Z:]]
    return got


def own_kernel(kx_ref, turned_ref, low_ref, high_ref):
    taps = kx_ref[HX : HX + BX]

    def along_x(t, carry):
        y0 = pl.multiple_of(t * 8, 8)
        planes = swapped(jnp.stack(times_rows(taps, turned_ref[pl.ds(y0, 8)]), axis=0))
        low_ref[:, pl.ds(y0, 8), :] = planes[:HX]
        high_ref[:, pl.ds(y0, 8), :] = planes[HX:]
        return carry

    lax.fori_loop(0, Y // 8, along_x, 0, unroll=8)


def back_from(kx_ref, ky_ref, kz_ref, measured_ref, blurred_ref, half_ref, edge_ref, peak_ref, outs):
    left_ref, right_ref, turned_ref = outs
    taps = jnp.concatenate([kx_ref[:HX], kx_ref[HX + BX :]], axis=0)

    def along_zy(q, carry):
        v = q // (BX // TP)
        ratio = (measured_ref[q].astype(F32) / blurred_ref[q]).astype(BF16)
        pairs = [
            jnp.concatenate([ratio[(i + j) * Y : (i + j + 1) * Y] for j in range(2)], axis=1)
            for i in range(0, TP, 2)
        ]
        rows = jnp.dot(
            jnp.concatenate(pairs, axis=0), kz_ref[v], preferred_element_type=F32
        ).astype(BF16)
        for i in range(0, TP, 2):
            pair = rows[i // 2 * Y : (i // 2 + 1) * Y]
            got = jnp.dot(ky_ref[v], pair, preferred_element_type=F32)
            for j in range(2):
                half_ref[q * TP + i + j] = got[:, j * Z : (j + 1) * Z]
        return carry

    lax.fori_loop(0, VIEWS_DEV * BX // TP, along_zy, 0, unroll=UNROLL)

    def along_x(t, carry):
        y0 = pl.multiple_of(t * 8, 8)
        data = swapped(half_ref[:, pl.ds(y0, 8), :])
        high = data.astype(BF16)
        low = (data - high.astype(F32)).astype(BF16)
        both = jnp.concatenate([high, low], axis=1)
        turned_ref[pl.ds(y0, 8)] = both
        planes = swapped(jnp.stack(times_rows(taps, both), axis=0))
        for i in range(2):
            part = planes[i * HX : (i + 1) * HX]
            edge_ref[i, :, pl.ds(y0, 8), :] = part
            peak_ref[i] = jnp.maximum(peak_ref[i], part)
        return carry

    peak_ref[...] = jnp.zeros(peak_ref.shape, F32)
    lax.fori_loop(0, Y // 8, along_x, 0, unroll=8)
    for i, ref in enumerate((left_ref, right_ref)):
        write_payload(ref, edge_ref.at[i], jnp.max(peak_ref[i], axis=1))


def first_blur_kernel(kx_ref, ky_ref, kz_ref, *refs):
    *parts, out_ref, half_ref = refs
    blur_into(kx_ref, ky_ref, kz_ref, parts, half_ref, out_ref)


def first_back_kernel(kx_ref, ky_ref, kz_ref, blurred_ref, *refs):
    tiles = refs[:SPAN]
    *outs, measured_ref, half_ref, edge_ref, peak_ref = refs[SPAN:]
    for k in range(SPAN):
        for c in range(CAP):
            code = tiles[k][CAP * TROWS :, :].astype(F32)[8 * c, 0].astype(jnp.int32)
            measured_ref[code] = tiles[k][c * TROWS : (c + 1) * TROWS, :]
    back_from(kx_ref, ky_ref, kz_ref, measured_ref, blurred_ref, half_ref, edge_ref, peak_ref, outs)


def sweep_kernel(*refs):
    fwd, back, parts = refs[0:3], refs[3:6], refs[6:10]
    measured_ref = refs[10]
    outs = refs[11:14]
    half_ref, edge_ref, peak_ref, blurred_ref = refs[14:]
    blur_into(*fwd, parts, half_ref, blurred_ref)
    back_from(*back, measured_ref, blurred_ref, half_ref, edge_ref, peak_ref, outs)


def join_kernel(own_ref, edge_ref, out_ref, sum_ref):
    scales = payload_scales(edge_ref)
    peaks = []
    for p in range(HX):
        plane = own_ref[p] + payload_plane(edge_ref, scales, p)
        sum_ref[p] = plane
        peaks.append(jnp.max(plane, axis=0, keepdims=True))
    write_payload(out_ref, sum_ref, jnp.concatenate(peaks, axis=0))


def update_planes(view_count, before_ref, own_ref, other_ref, out_refs):
    own, other = payload_scales(own_ref), payload_scales(other_ref)
    for p in range(HX):
        total = payload_plane(own_ref, own, p) + payload_plane(other_ref, other, p)
        plane = before_ref[p] * total * (1.0 / view_count)
        for ref in out_refs:
            ref[p] = plane.astype(ref.dtype)


def update_kernel(view_count, before_ref, own_ref, other_ref, *out_refs):
    update_planes(view_count, before_ref, own_ref, other_ref, out_refs)


def last_kernel(view_count, low_ref, high_ref, *refs):
    *payloads, out_ref, plane_ref, sems = refs
    copies = []
    for i, before_ref in enumerate((low_ref, high_ref)):
        own_ref, other_ref = payloads[2 * i : 2 * i + 2]
        part = pl.ds(i * HX, HX)
        update_planes(view_count, before_ref, own_ref, other_ref, (plane_ref.at[part],))
        copies.append(pltpu.make_async_copy(plane_ref.at[part], out_ref.at[part], sems.at[i]))
        copies[-1].start()
    for copy in copies:
        copy.wait()


VM = pl.BlockSpec(memory_space=pltpu.VMEM)
BLURRED = (VIEWS_DEV * BX // TP, TROWS, Z)
HALF_SHAPE = (VIEWS_DEV * BX, Y, Z)
PAYLOAD = jax.ShapeDtypeStruct((HX * Y + HX, Z), I16)
OWN = jax.ShapeDtypeStruct((HX, Y, Z), F32)
CONTRIB = [PAYLOAD, PAYLOAD, jax.ShapeDtypeStruct((Y, 2 * VIEWS_DEV * BX, Z), BF16)]
BLUR_SCRATCH = [pltpu.VMEM(HALF_SHAPE, BF16)]
BACK_SCRATCH = [
    pltpu.VMEM(HALF_SHAPE, F32),
    pltpu.VMEM((2, HX, Y, Z), F32),
    pltpu.VMEM((2, HX, 8, Z), F32),
]


def call(kernel, name, operands, out_shape, scratch, flops, vmem=6, out=VM):
    return pl.pallas_call(
        kernel,
        out_shape=out_shape,
        in_specs=[VM] * len(operands),
        out_specs=jax.tree.map(lambda _: out, out_shape),
        scratch_shapes=scratch,
        compiler_params=pltpu.CompilerParams(vmem_limit_bytes=vmem * MIB),
        cost_estimate=pl.CostEstimate(flops=flops, bytes_accessed=12 << 20, transcendentals=0),
        name=name,
    )(*operands)


def neighbours(low, high):
    size = lax.axis_size("block")
    up = [(i, i + 1) for i in range(size - 1)]
    down = [(j, i) for i, j in up]
    return lax.ppermute(high, "block", up), lax.ppermute(low, "block", down)


def exchanged(contributions, back_x):
    left, right, turned = contributions
    arrived = neighbours(left, right)
    owns = call(own_kernel, "own", (back_x, turned), [OWN, OWN], [], 1 << 30, 12)
    pairs = []
    for own, edge in zip(owns, arrived):
        payload = call(join_kernel, "join", (own, edge), PAYLOAD, [pltpu.VMEM(OWN.shape, F32)], 1 << 20)
        pairs.append((payload, lax.ppermute(payload, "view", [(0, 1), (1, 0)])))
    return pairs


def shards(estimate, view_tiles, tile_dest, psf_taps):
    view_count = psf_taps.shape[0] * lax.axis_size("view")
    blocks = lax.axis_size("block")
    packed = pack_tiles(view_tiles, tile_dest)
    arrived = list(packed)

    def route(steps):
        for by in steps:
            perm = [(i, (i + by) % blocks) for i in range(blocks)]
            arrived[by + SPAN // 2] = lax.ppermute(packed[by + SPAN // 2], "block", perm)

    planes = estimate.astype(BF16)
    low, high = planes[:HX], planes[HX:]
    left, right = neighbours(low, high)
    route(EARLY)
    fwd, back = blur_matrices(psf_taps)
    blurred = call(
        first_blur_kernel,
        "first_blur",
        (*fwd, left, low, high, right),
        jax.ShapeDtypeStruct(BLURRED, F32),
        BLUR_SCRATCH,
        6 << 30,
        18,
    )
    packed, blurred = lax.optimization_barrier((packed, blurred))
    route(LATE)
    *contributions, measured = call(
        first_back_kernel,
        "first_back",
        (*back, blurred, *arrived),
        [*CONTRIB, jax.ShapeDtypeStruct((VIEWS_DEV * BX // TP, TROWS, Z), BF16)],
        BACK_SCRATCH,
        8 << 30,
        32,
    )
    halves = []
    for i, (own, other) in enumerate(exchanged(contributions, back[0])):
        halves.append(
            call(
                functools.partial(update_kernel, view_count),
                "update",
                (estimate[i * HX : (i + 1) * HX], own, other),
                [OWN, jax.ShapeDtypeStruct(OWN.shape, BF16)],
                [],
                1 << 20,
            )
        )
    (low, low_planes), (high, high_planes) = halves
    left, right = neighbours(low_planes, high_planes)
    contributions = call(
        sweep_kernel,
        "sweep",
        (*fwd, *back, left, low_planes, high_planes, right, measured),
        CONTRIB,
        [*BACK_SCRATCH, pltpu.VMEM(BLURRED, F32)],
        14 << 30,
        34,
    )
    payloads = [payload for pair in exchanged(contributions, back[0]) for payload in pair]
    return call(
        functools.partial(last_kernel, view_count),
        "last_update",
        (low, high, *payloads),
        jax.ShapeDtypeStruct(estimate.shape, F32),
        [pltpu.VMEM(estimate.shape, F32), pltpu.SemaphoreType.DMA((2,))],
        1 << 20,
        10,
        pl.BlockSpec(memory_space=pl.ANY),
    )


def solution(mesh):
    return jax.shard_map(
        shards,
        mesh=mesh,
        in_specs=(
            P("block", None, None),
            P("view", "block", None, None, None),
            P("view", "block", None),
            P("view", None, None),
        ),
        out_specs=P("block", None, None),
        check_vma=False,
    )
```

```python
import functools

import jax
import jax.numpy as jnp
from jax import lax
from jax.experimental import pallas as pl
from jax.experimental.pallas import tpu as pltpu
from jax.sharding import PartitionSpec as P

TAPS = 31
HALF = TAPS // 2
BX = 32
HX = 16
EX = BX + 2 * HX
Y = 128
Z = 128
LANES = 128
VIEWS_DEV = 3
ITERS = 2
CAP = 2
SPAN = 12
TP = 4
SLOTS = SPAN * CAP
TROWS = TP * Y
PROWS = CAP * TROWS + 16
SUB = 16
F32 = jnp.float32
BF16 = jnp.bfloat16
I16 = jnp.int16
MIB = 1 << 20
UNROLL = 12
EARLY = (-6, 5, -5, 4, -4, 3, -3)
LATE = (2, -2, 1, -1)


def toeplitz(row, rows, shift, low, high):
    turned = pltpu.roll(
        jnp.broadcast_to(row, (rows, LANES)), shift % LANES, 1, stride=1, stride_axis=0
    )
    lag = lax.broadcasted_iota(jnp.int32, (rows, LANES), 1) - lax.broadcasted_iota(
        jnp.int32, (rows, LANES), 0
    )
    return jnp.where((lag >= low) & (lag <= high), turned, 0.0)


def prepare_kernel(psf_ref, *refs):
    *outs, taps_ref, turned_ref = refs
    fwd_x_ref, fwd_y_ref, fwd_z_ref, back_x_ref, back_y_ref, back_z_ref = outs
    dims = psf_ref.shape[1]
    taps_ref[...] = jnp.zeros(taps_ref.shape, F32)
    for v in range(VIEWS_DEV):
        taps = psf_ref[v]
        taps_ref[v * dims : (v + 1) * dims, :TAPS] = taps / jnp.sum(taps, axis=1, keepdims=True)
    turned_ref[...] = jnp.transpose(taps_ref[...])
    left_over = jnp.zeros((1, LANES), F32)
    for a in range(TAPS):
        wanted = turned_ref[a : a + 1, :] + left_over
        near = wanted.astype(BF16).astype(F32)
        left_over = wanted - near
        turned_ref[a : a + 1, :] = near
    taps_ref[...] = jnp.transpose(turned_ref[...])
    for a in range(TAPS):
        turned_ref[TAPS + 1 + a : TAPS + 2 + a, :] = turned_ref[TAPS - 1 - a : TAPS - a, :]
    turned_ref[:TAPS, :] = turned_ref[TAPS + 1 : 2 * TAPS + 1, :]
    turned_ref[TAPS:, :] = jnp.zeros((LANES - TAPS, LANES), F32)
    turned_ref[...] = jnp.transpose(turned_ref[...])
    wide = []
    for v in range(VIEWS_DEV):
        ahead = [taps_ref[v * dims + d : v * dims + d + 1, :] for d in range(dims)]
        behind = [turned_ref[v * dims + d : v * dims + d + 1, :] for d in range(dims)]
        wide.append(toeplitz(ahead[0], BX, 1, 1, TAPS))
        for ref, row in ((fwd_y_ref, ahead[1]), (back_y_ref, behind[1])):
            ref[v] = toeplitz(row, LANES, -HALF, -HALF, HALF).astype(BF16)
        for ref, row in ((fwd_z_ref, behind[2]), (back_z_ref, ahead[2])):
            block = toeplitz(row, LANES, -HALF, -HALF, HALF).astype(BF16)
            ref[v] = jnp.zeros(ref.shape[1:], BF16)
            ref[v, :LANES, :LANES] = block
            ref[v, LANES:, LANES:] = block
    along = jnp.concatenate(wide, axis=0)
    fwd_x_ref[...] = along[:, :EX].astype(BF16)
    full = jnp.concatenate([along, jnp.zeros((LANES - VIEWS_DEV * BX, LANES), F32)], axis=0)
    across = jnp.transpose(full)[:EX, : VIEWS_DEV * BX].astype(BF16)
    back_x_ref[...] = jnp.concatenate([across, across], axis=1)


def blur_matrices(psf_taps):
    square = jax.ShapeDtypeStruct((VIEWS_DEV, LANES, LANES), BF16)
    double = jax.ShapeDtypeStruct((VIEWS_DEV, 2 * LANES, 2 * LANES), BF16)
    shapes = [
        jax.ShapeDtypeStruct((VIEWS_DEV * BX, EX), BF16),
        square,
        double,
        jax.ShapeDtypeStruct((EX, 2 * VIEWS_DEV * BX), BF16),
        square,
        double,
    ]
    scratch = [pltpu.VMEM((LANES, LANES), F32)] * 2
    matrices = call(prepare_kernel, "prepare", (psf_taps,), shapes, scratch, 1 << 20)
    return matrices[:3], matrices[3:]


def pack_kernel(me_ref, dest_ref, tiles_ref, *refs):
    outs, (order_ref, count_ref) = refs[:SPAN], refs[SPAN:]
    me = me_ref[0]
    for k in range(SPAN):
        count_ref[k] = 0
    for n in range(SLOTS):
        step = lax.rem(dest_ref[n, 0] - me + SPAN // 2 + 64, 64)
        rank = count_ref[step]
        count_ref[step] = rank + 1
        order_ref[step * CAP + rank] = n
    for k in range(SPAN):
        codes = []
        for c in range(CAP):
            n = order_ref[k * CAP + c]
            outs[k][c * TROWS : (c + 1) * TROWS, :] = tiles_ref[n]
            code = dest_ref[n, 1] * (BX // TP) + dest_ref[n, 2]
            codes.append(jnp.full((8, Z), code, jnp.int32).astype(F32))
        outs[k][CAP * TROWS :, :] = jnp.concatenate(codes, axis=0).astype(BF16)


def pack_tiles(view_tiles, tile_dest):
    me = lax.axis_index("block").astype(jnp.int32).reshape(1)
    return pl.pallas_call(
        pack_kernel,
        out_shape=[jax.ShapeDtypeStruct((PROWS, Z), BF16)] * SPAN,
        in_specs=[
            pl.BlockSpec(memory_space=pltpu.SMEM),
            pl.BlockSpec(memory_space=pltpu.SMEM),
            pl.BlockSpec(memory_space=pltpu.VMEM),
        ],
        out_specs=[pl.BlockSpec(memory_space=pltpu.VMEM)] * SPAN,
        scratch_shapes=[pltpu.SMEM((SLOTS,), jnp.int32), pltpu.SMEM((SPAN,), jnp.int32)],
        compiler_params=pltpu.CompilerParams(vmem_limit_bytes=8 * MIB),
        cost_estimate=pl.CostEstimate(flops=0, bytes_accessed=2 * SLOTS * TROWS * Z * 2, transcendentals=0),
        name="pack_tiles",
    )(me, tile_dest[0], view_tiles.reshape(SLOTS, TROWS, Z))


STEPS = (64, 32, 16, 8, 4, 2, 1)
OFFSET = 64


def column_codes(peak):
    bound = peak * (2.0**-15 * (1 + 2.0**-12))
    scale = jnp.full(peak.shape, 2.0 ** (1 - OFFSET), F32)
    shrink = jnp.full(peak.shape, 2.0 ** (OFFSET - 1), F32)
    power = jnp.full(peak.shape, 1.0 - OFFSET, F32)
    for step in STEPS:
        larger = scale * 2.0 ** (step - 1) <= bound
        scale = jnp.where(larger, scale * 2.0**step, scale)
        shrink = jnp.where(larger, shrink * 2.0**-step, shrink)
        power = jnp.where(larger, power + step, power)
    return shrink, power


def column_scales(power):
    left = power + OFFSET
    scale = jnp.full(power.shape, 2.0**-OFFSET, F32)
    for step in STEPS:
        larger = left >= step
        scale = jnp.where(larger, scale * 2.0**step, scale)
        left = jnp.where(larger, left - step, left)
    return scale


def to_codes(values):
    return jnp.round(values).astype(jnp.int32).astype(I16)


def from_codes(codes):
    return codes.astype(jnp.int32).astype(F32)


def write_payload(ref, planes, peak):
    shrink, power = column_codes(peak)
    for p in range(HX):
        ref[p * Y : (p + 1) * Y, :] = to_codes(planes[p] * shrink[p : p + 1])
    ref[HX * Y :, :] = power.astype(jnp.int32).astype(I16)


def payload_scales(ref):
    return column_scales(from_codes(ref[HX * Y :, :]))


def payload_plane(ref, scales, p):
    return from_codes(ref[p * Y : (p + 1) * Y, :]) * scales[p : p + 1]


def swapped(block):
    return jnp.transpose(block, (1, 0, 2))


def blur_into(kx_ref, ky_ref, kz_ref, parts, half_ref, out_ref):
    def along_x(t, carry):
        y0 = pl.multiple_of(t * SUB, SUB)
        data = jnp.concatenate([ref[:, pl.ds(y0, SUB), :] for ref in parts], axis=0).astype(F32)
        planes = []
        for h in range(0, SUB, 8):
            rows = swapped(data[:, h : h + 8]).astype(BF16)
            outs = []
            for j in range(0, 8, 2):
                pair = jnp.concatenate([rows[j], rows[j + 1]], axis=1)
                got = jnp.dot(kx_ref[...], pair, preferred_element_type=F32)
                outs += [got[:, :Z], got[:, Z:]]
            planes.append(swapped(jnp.stack(outs, axis=0)))
        half_ref[:, pl.ds(y0, SUB), :] = jnp.concatenate(planes, axis=1).astype(half_ref.dtype)
        return carry

    lax.fori_loop(0, Y // SUB, along_x, 0, unroll=2)

    def along_yz(q, carry):
        v = q // (BX // TP)
        outs = []
        for i in range(0, TP, 2):
            pair = jnp.concatenate([half_ref[q * TP + i + j].astype(BF16) for j in range(2)], axis=1)
            outs.append(jnp.dot(ky_ref[v], pair, preferred_element_type=F32).astype(BF16))
        got = jnp.dot(jnp.concatenate(outs, axis=0), kz_ref[v], preferred_element_type=F32)
        for i in range(TP):
            rows, lanes = i // 2 * Y, i % 2 * Z
            out_ref[q, i * Y : (i + 1) * Y, :] = got[rows : rows + Y, lanes : lanes + Z]
        return carry

    lax.fori_loop(0, VIEWS_DEV * BX // TP, along_yz, 0, unroll=UNROLL)


def times_rows(taps, rows):
    got = []
    for j in range(0, 8, 2):
        pair = jnp.concatenate([rows[j], rows[j + 1]], axis=1)
        both = jnp.dot(taps, pair, preferred_element_type=F32)
        got += [both[:, :Z], both[:, Z:]]
    return got


def own_kernel(kx_ref, turned_ref, low_ref, high_ref):
    taps = kx_ref[HX : HX + BX]

    def along_x(t, carry):
        y0 = pl.multiple_of(t * 8, 8)
        planes = swapped(jnp.stack(times_rows(taps, turned_ref[pl.ds(y0, 8)]), axis=0))
        low_ref[:, pl.ds(y0, 8), :] = planes[:HX]
        high_ref[:, pl.ds(y0, 8), :] = planes[HX:]
        return carry

    lax.fori_loop(0, Y // 8, along_x, 0, unroll=8)


def back_from(kx_ref, ky_ref, kz_ref, measured_ref, blurred_ref, half_ref, edge_ref, peak_ref, outs):
    left_ref, right_ref, turned_ref = outs
    taps = jnp.concatenate([kx_ref[:HX], kx_ref[HX + BX :]], axis=0)

    def along_zy(q, carry):
        v = q // (BX // TP)
        ratio = (measured_ref[q].astype(F32) / blurred_ref[q]).astype(BF16)
        pairs = [
            jnp.concatenate([ratio[(i + j) * Y : (i + j + 1) * Y] for j in range(2)], axis=1)
            for i in range(0, TP, 2)
        ]
        rows = jnp.dot(
            jnp.concatenate(pairs, axis=0), kz_ref[v], preferred_element_type=F32
        ).astype(BF16)
        for i in range(0, TP, 2):
            pair = rows[i // 2 * Y : (i // 2 + 1) * Y]
            got = jnp.dot(ky_ref[v], pair, preferred_element_type=F32)
            for j in range(2):
                half_ref[q * TP + i + j] = got[:, j * Z : (j + 1) * Z]
        return carry

    lax.fori_loop(0, VIEWS_DEV * BX // TP, along_zy, 0, unroll=UNROLL)

    def along_x(t, carry):
        y0 = pl.multiple_of(t * 8, 8)
        data = swapped(half_ref[:, pl.ds(y0, 8), :])
        high = data.astype(BF16)
        low = (data - high.astype(F32)).astype(BF16)
        both = jnp.concatenate([high, low], axis=1)
        turned_ref[pl.ds(y0, 8)] = both
        planes = swapped(jnp.stack(times_rows(taps, both), axis=0))
        for i in range(2):
            part = planes[i * HX : (i + 1) * HX]
            edge_ref[i, :, pl.ds(y0, 8), :] = part
            peak_ref[i] = jnp.maximum(peak_ref[i], part)
        return carry

    peak_ref[...] = jnp.zeros(peak_ref.shape, F32)
    lax.fori_loop(0, Y // 8, along_x, 0, unroll=8)
    for i, ref in enumerate((left_ref, right_ref)):
        write_payload(ref, edge_ref.at[i], jnp.max(peak_ref[i], axis=1))


def first_blur_kernel(kx_ref, ky_ref, kz_ref, *refs):
    *parts, out_ref, half_ref = refs
    blur_into(kx_ref, ky_ref, kz_ref, parts, half_ref, out_ref)


def first_back_kernel(kx_ref, ky_ref, kz_ref, blurred_ref, *refs):
    tiles = refs[:SPAN]
    *outs, measured_ref, half_ref, edge_ref, peak_ref = refs[SPAN:]
    for k in range(SPAN):
        for c in range(CAP):
            code = tiles[k][CAP * TROWS :, :].astype(F32)[8 * c, 0].astype(jnp.int32)
            measured_ref[code] = tiles[k][c * TROWS : (c + 1) * TROWS, :]
    back_from(kx_ref, ky_ref, kz_ref, measured_ref, blurred_ref, half_ref, edge_ref, peak_ref, outs)


def sweep_kernel(*refs):
    fwd, back, parts = refs[0:3], refs[3:6], refs[6:10]
    measured_ref = refs[10]
    outs = refs[11:14]
    half_ref, edge_ref, peak_ref, blurred_ref = refs[14:]
    blur_into(*fwd, parts, half_ref, blurred_ref)
    back_from(*back, measured_ref, blurred_ref, half_ref, edge_ref, peak_ref, outs)


def join_kernel(own_ref, edge_ref, out_ref, sum_ref):
    scales = payload_scales(edge_ref)
    peaks = []
    for p in range(HX):
        plane = own_ref[p] + payload_plane(edge_ref, scales, p)
        sum_ref[p] = plane
        peaks.append(jnp.max(plane, axis=0, keepdims=True))
    write_payload(out_ref, sum_ref, jnp.concatenate(peaks, axis=0))


def update_planes(view_count, before_ref, own_ref, other_ref, out_refs):
    own, other = payload_scales(own_ref), payload_scales(other_ref)
    for p in range(HX):
        total = payload_plane(own_ref, own, p) + payload_plane(other_ref, other, p)
        plane = before_ref[p] * total * (1.0 / view_count)
        for ref in out_refs:
            ref[p] = plane.astype(ref.dtype)


def update_kernel(view_count, before_ref, own_ref, other_ref, *out_refs):
    update_planes(view_count, before_ref, own_ref, other_ref, out_refs)


def low_kernel(view_count, before_ref, own_ref, other_ref, out_ref):
    update_planes(view_count, before_ref, own_ref, other_ref, (out_ref,))


def last_kernel(view_count, low_ref, before_ref, own_ref, other_ref, out_ref, high_ref, sems):
    copies = [
        pltpu.make_async_copy(ref, out_ref.at[pl.ds(i * HX, HX)], sems.at[i])
        for i, ref in enumerate((low_ref, high_ref))
    ]
    copies[0].start()
    update_planes(view_count, before_ref, own_ref, other_ref, (high_ref,))
    copies[1].start()
    for copy in copies:
        copy.wait()


VM = pl.BlockSpec(memory_space=pltpu.VMEM)
BLURRED = (VIEWS_DEV * BX // TP, TROWS, Z)
HALF_SHAPE = (VIEWS_DEV * BX, Y, Z)
PAYLOAD = jax.ShapeDtypeStruct((HX * Y + HX, Z), I16)
OWN = jax.ShapeDtypeStruct((HX, Y, Z), F32)
CONTRIB = [PAYLOAD, PAYLOAD, jax.ShapeDtypeStruct((Y, 2 * VIEWS_DEV * BX, Z), BF16)]
BLUR_SCRATCH = [pltpu.VMEM(HALF_SHAPE, BF16)]
BACK_SCRATCH = [
    pltpu.VMEM(HALF_SHAPE, F32),
    pltpu.VMEM((2, HX, Y, Z), F32),
    pltpu.VMEM((2, HX, 8, Z), F32),
]


def call(kernel, name, operands, out_shape, scratch, flops, vmem=6, out=VM):
    return pl.pallas_call(
        kernel,
        out_shape=out_shape,
        in_specs=[VM] * len(operands),
        out_specs=jax.tree.map(lambda _: out, out_shape),
        scratch_shapes=scratch,
        compiler_params=pltpu.CompilerParams(vmem_limit_bytes=vmem * MIB),
        cost_estimate=pl.CostEstimate(flops=flops, bytes_accessed=12 << 20, transcendentals=0),
        name=name,
    )(*operands)


def neighbours(low, high):
    size = lax.axis_size("block")
    up = [(i, i + 1) for i in range(size - 1)]
    down = [(j, i) for i, j in up]
    return lax.ppermute(high, "block", up), lax.ppermute(low, "block", down)


def exchanged(contributions, back_x):
    left, right, turned = contributions
    arrived = neighbours(left, right)
    owns = call(own_kernel, "own", (back_x, turned), [OWN, OWN], [], 1 << 30, 12)
    pairs = []
    for own, edge in zip(owns, arrived):
        payload = call(join_kernel, "join", (own, edge), PAYLOAD, [pltpu.VMEM(OWN.shape, F32)], 1 << 20)
        pairs.append((payload, lax.ppermute(payload, "view", [(0, 1), (1, 0)])))
    return pairs


def shards(estimate, view_tiles, tile_dest, psf_taps):
    view_count = psf_taps.shape[0] * lax.axis_size("view")
    blocks = lax.axis_size("block")
    packed = pack_tiles(view_tiles, tile_dest)
    arrived = list(packed)

    def route(steps):
        for by in steps:
            perm = [(i, (i + by) % blocks) for i in range(blocks)]
            arrived[by + SPAN // 2] = lax.ppermute(packed[by + SPAN // 2], "block", perm)

    planes = estimate.astype(BF16)
    low, high = planes[:HX], planes[HX:]
    left, right = neighbours(low, high)
    route(EARLY)
    fwd, back = blur_matrices(psf_taps)
    blurred = call(
        first_blur_kernel,
        "first_blur",
        (*fwd, left, low, high, right),
        jax.ShapeDtypeStruct(BLURRED, F32),
        BLUR_SCRATCH,
        6 << 30,
        18,
    )
    packed, blurred = lax.optimization_barrier((packed, blurred))
    route(LATE)
    *contributions, measured = call(
        first_back_kernel,
        "first_back",
        (*back, blurred, *arrived),
        [*CONTRIB, jax.ShapeDtypeStruct((VIEWS_DEV * BX // TP, TROWS, Z), BF16)],
        BACK_SCRATCH,
        8 << 30,
        32,
    )
    halves = []
    for i, (own, other) in enumerate(exchanged(contributions, back[0])):
        halves.append(
            call(
                functools.partial(update_kernel, view_count),
                "update",
                (estimate[i * HX : (i + 1) * HX], own, other),
                [OWN, jax.ShapeDtypeStruct(OWN.shape, BF16)],
                [],
                1 << 20,
            )
        )
    (low, low_planes), (high, high_planes) = halves
    left, right = neighbours(low_planes, high_planes)
    contributions = call(
        sweep_kernel,
        "sweep",
        (*fwd, *back, left, low_planes, high_planes, right, measured),
        CONTRIB,
        [*BACK_SCRATCH, pltpu.VMEM(BLURRED, F32)],
        14 << 30,
        34,
    )
    low_pair, high_pair = exchanged(contributions, back[0])
    low = call(
        functools.partial(low_kernel, view_count), "low_update", (low, *low_pair), OWN, [], 1 << 20
    )
    return call(
        functools.partial(last_kernel, view_count),
        "last_update",
        (low, high, *high_pair),
        jax.ShapeDtypeStruct(estimate.shape, F32),
        [pltpu.VMEM(OWN.shape, F32), pltpu.SemaphoreType.DMA((2,))],
        1 << 20,
        10,
        pl.BlockSpec(memory_space=pl.ANY),
    )


def solution(mesh):
    return jax.shard_map(
        shards,
        mesh=mesh,
        in_specs=(
            P("block", None, None),
            P("view", "block", None, None, None),
            P("view", "block", None),
            P("view", None, None),
        ),
        out_specs=P("block", None, None),
        check_vma=False,
    )
```
